512 devices in a mesh: seq: 64 (over y, z), head: 8 (over x, core).
Axes of the slice: x: 4, y: 8, z: 8, core: 2. Of those that a mesh axis runs over, the one named last changes fastest.
Arguments:
- queries: bfloat16 [16384, 4096], P(('seq', 'head'))
- key_values: bfloat16 [16384, 2, 1024], P(('seq', 'head'))
- gate_logits: bfloat16 [16384, 4096], P(('seq', 'head')), may hold values from -6 to 6
- vertical_blocks: int32 [32, 16], replicated, may hold values from 0 to 255, as said below
- slash_offsets: int32 [32, 8], replicated, may hold values from 0 to 8, as said below
- slash_count: int32 [32], replicated, may hold values from 2 to 8, as said below
Outputs:
- gated: bfloat16 [16384, 4096], P(('seq', 'head'))
The draws below stay inside these ranges and needn't reach their ends.
Inputs may be any that keep to these rules, and one draw needn't show every extreme that they name: `slash_count`: between 2 and 8; the largest and the smallest are reached. Heads are ranked by (slash_count[h], h) ascending, and rank r goes to head group (r % 8) if (r // 8) is even, else to group 8 - 1 - (r % 8). For each head, slash_offsets[h, 0] = 0 and the 8 offsets are distinct; the largest possible offset is used by some head. `vertical_blocks`: each head's 16 blocks lie in distinct token shards of 256 tokens (block b is in shard b // 4); the heads of one group, as defined with slash_count, have at most 1 vertical blocks in one shard together, and exactly 1 in some shard. The first and the last block of the stretch are used by some head.
All inputs are finite; a program needn't handle non-finite values.
Results may differ from the reference program's by a relative error of at most 0.0057.
Values may be sent and summed in bfloat16 or wider, within the bound.
No kernel may reach another device: no remote copies, remote signals or barrier semaphores. Data moves between devices by JAX's collectives and lax.ppermute only.
A program may use at most 64 MiB of HBM per device.

```python
import jax
import jax.numpy as jnp
from jax import lax

H = 32
KVH = 8
DH = 128
BLOCK = 64
NV = 16
NS = 8
TOKENS = 16384
BLOCKS_DEV = 4
SPAN = 9
N_SEQ = 64
N_HEAD = 8


def density_counts(key):
    counts = jax.random.randint(jax.random.fold_in(key, 11), (H,), 2, NS + 1)
    chosen_idx = jax.random.permutation(jax.random.fold_in(key, 12), H)
    counts = counts.at[chosen_idx[0]].set(NS).at[chosen_idx[1]].set(2)
    return counts.astype(jnp.int32)


def group_order(counts):
    group_size = H // N_HEAD
    ranking = jnp.argsort(counts * H + jnp.arange(H, dtype=jnp.int32), stable=True).astype(jnp.int32)
    index = jnp.arange(H, dtype=jnp.int32)
    group = index // group_size
    within = index % group_size
    rank_of = within * N_HEAD + jnp.where(within % 2 == 0, group, N_HEAD - 1 - group)
    return ranking[rank_of]


def draw_slash_count(key, part):
    return density_counts(key)


def draw_vertical_blocks(key, part):
    counts = density_counts(key)
    head_order = group_order(counts)
    group_size = H // N_HEAD
    subkeys = jax.random.split(jax.random.fold_in(key, 21), N_HEAD)
    orders_tab = jax.vmap(lambda subkey: jax.random.permutation(subkey, N_SEQ))(subkeys)
    first_row = jnp.concatenate([jnp.array([N_SEQ - 1, 0], dtype=orders_tab.dtype), jax.random.permutation(jax.random.fold_in(key, 23), N_SEQ - 2).astype(orders_tab.dtype) + 1])
    orders_tab = orders_tab.at[0].set(first_row)
    index = jnp.arange(H, dtype=jnp.int32)
    group = index // group_size
    within = index % group_size
    place = (within[:, None] * NV + jnp.arange(NV, dtype=jnp.int32)[None, :]) % N_SEQ
    device_of = orders_tab[group[:, None], place]
    offset_in = jax.random.randint(jax.random.fold_in(key, 22), (H, NV), 0, BLOCKS_DEV)
    offset_in = offset_in.at[0, 0].set(BLOCKS_DEV - 1).at[0, 1].set(0)
    blocks = (device_of * BLOCKS_DEV + offset_in).astype(jnp.int32)
    return jnp.zeros((H, NV), jnp.int32).at[head_order].set(blocks)


def draw_slash_offsets(key, part):
    subkeys = jax.random.split(jax.random.fold_in(key, 31), H)
    orders_tab = jax.vmap(lambda subkey: jax.random.permutation(subkey, SPAN - 1))(subkeys) + 1
    chosen = jax.random.randint(jax.random.fold_in(key, 32), (), 0, H)
    first_col = orders_tab[:, :1]
    swapped = jnp.where(orders_tab == SPAN - 1, first_col, orders_tab)
    swapped = swapped.at[:, 0].set(SPAN - 1)
    orders_tab = jnp.where((jnp.arange(H) == chosen)[:, None], swapped, orders_tab)
    zeros_col = jnp.zeros((H, 1), orders_tab.dtype)
    return jnp.concatenate([zeros_col, orders_tab[:, :NS - 1]], axis=1).astype(jnp.int32)


def draw_queries(key, part):
    values = jnp.clip(1.5 * jax.random.normal(jax.random.fold_in(key, 1), (TOKENS, H, DH), jnp.float32), -6.0, 6.0)
    return values.reshape(TOKENS, H * DH).astype(jnp.bfloat16)


def draw_key_values(key, part):
    key_part = jnp.clip(jax.random.normal(jax.random.fold_in(key, 2), (TOKENS, KVH, DH), jnp.float32), -6.0, 6.0)
    value_part = jnp.clip(2.0 * jax.random.normal(jax.random.fold_in(key, 3), (TOKENS, KVH, DH), jnp.float32), -12.0, 12.0)
    stacked = jnp.stack([key_part, value_part], axis=1)
    return stacked.reshape(TOKENS, 2, KVH * DH).astype(jnp.bfloat16)


def block_levels(own_key, shape, pieces, least, high):
    level = 1.0
    for dim, shards_of in pieces:
        heights = jax.random.uniform(jax.random.fold_in(jax.random.fold_in(own_key, 6), dim), (shards_of,), jnp.float32, least / len(pieces), high / len(pieces))
        level = level * jnp.repeat(jnp.exp(heights), shape[dim] // shards_of).reshape((-1,) + (1,) * (len(shape) - 1 - dim))
    return level


def scatter_about(own_key, shape, scale, most, pieces=(), held_as=jnp.bfloat16):
    gain = block_levels(own_key, shape, pieces, -0.22, 0.18) if pieces else 1.0
    drawn = jax.random.normal(own_key, shape, jnp.float32) * scale * gain
    return jnp.minimum(jnp.maximum(drawn, -most), most).astype(held_as)


def setup_inputs(seed: int = 0) -> dict:
    streams_of = jax.random.split(jax.random.key(seed), 7)
    return {
        "queries": draw_queries(jax.random.fold_in(streams_of[6], 71), 0),
        "key_values": draw_key_values(jax.random.fold_in(streams_of[6], 71), 0),
        "gate_logits": scatter_about(streams_of[2], (TOKENS, H * DH), 1.0, 6.0, ((0, 512),)),
        "vertical_blocks": draw_vertical_blocks(jax.random.fold_in(streams_of[6], 71), 0),
        "slash_offsets": draw_slash_offsets(jax.random.fold_in(streams_of[6], 71), 0),
        "slash_count": draw_slash_count(jax.random.fold_in(streams_of[6], 71), 0),
    }


def block_attend(q_rows, vert_keys, vert_vals, vert_ids, vert_live, slash_keys, slash_vals, offsets, slash_live, block_index):
    head_width = q_rows.shape[-1]
    score_scale = head_width ** -0.5
    positions = jnp.arange(q_rows.shape[0], dtype=jnp.int32)
    causal = positions[None, :] <= positions[:, None]
    vert_scores = jnp.einsum("qd,skd->qsk", q_rows.astype(jnp.float32), vert_keys.astype(jnp.float32)) * score_scale
    slash_scores = jnp.einsum("qd,nkd->qnk", q_rows.astype(jnp.float32), slash_keys.astype(jnp.float32)) * score_scale
    distance = block_index - vert_ids
    on_slash = jnp.any((distance[:, None] == offsets[None, :]) & slash_live[None, :], axis=1)
    vert_ok = vert_live & (vert_ids >= 0) & (vert_ids <= block_index) & jnp.logical_not(on_slash)
    vert_mask = vert_ok[None, :, None] & ((vert_ids < block_index)[None, :, None] | causal[:, None, :])
    slash_ok = slash_live & (block_index - offsets >= 0)
    slash_mask = slash_ok[None, :, None] & ((offsets > 0)[None, :, None] | causal[:, None, :])
    vert_scores = jnp.where(vert_mask, vert_scores, -jnp.inf)
    slash_scores = jnp.where(slash_mask, slash_scores, -jnp.inf)
    row_max = jnp.maximum(jnp.max(vert_scores, axis=(1, 2)), jnp.max(slash_scores, axis=(1, 2)))
    vert_exp = jnp.exp(vert_scores - row_max[:, None, None])
    slash_exp = jnp.exp(slash_scores - row_max[:, None, None])
    row_total = jnp.sum(vert_exp, axis=(1, 2)) + jnp.sum(slash_exp, axis=(1, 2))
    vert_weight = (vert_exp / row_total[:, None, None]).astype(jnp.bfloat16)
    slash_weight = (slash_exp / row_total[:, None, None]).astype(jnp.bfloat16)
    result = jnp.einsum("qsk,skd->qd", vert_weight.astype(jnp.float32), vert_vals.astype(jnp.float32))
    result = result + jnp.einsum("qnk,nkd->qd", slash_weight.astype(jnp.float32), slash_vals.astype(jnp.float32))
    return result.astype(jnp.bfloat16)


def reference(queries, key_values, gate_logits, vertical_blocks, slash_offsets, slash_count):
    block_count = TOKENS // BLOCK
    query_heads = queries.reshape(block_count, BLOCK, H, DH).transpose(2, 0, 1, 3)
    pairs = key_values.reshape(block_count, BLOCK, 2, KVH, DH).transpose(2, 3, 0, 1, 4)
    head_ratio = H // KVH
    block_ids = jnp.arange(block_count, dtype=jnp.int32)

    def one_head(head):
        q_head = query_heads[head]
        key_head = pairs[0, head // head_ratio]
        value_head = pairs[1, head // head_ratio]
        vert_ids = vertical_blocks[head].astype(jnp.int32)
        offsets = slash_offsets[head].astype(jnp.int32)
        slash_live = jnp.arange(NS, dtype=jnp.int32) < slash_count[head]
        vert_keys = key_head[vert_ids]
        vert_vals = value_head[vert_ids]
        slash_index = jnp.maximum(block_ids[:, None] - offsets[None, :], 0).astype(jnp.int32)
        slash_keys = key_head[slash_index]
        slash_vals = value_head[slash_index]
        vert_live = jnp.ones((NV,), dtype=bool)
        return jax.vmap(block_attend, in_axes=(0, None, None, None, None, 0, 0, None, None, 0))(
            q_head, vert_keys, vert_vals, vert_ids, vert_live, slash_keys, slash_vals, offsets, slash_live, block_ids)

    attended = lax.map(one_head, jnp.arange(H, dtype=jnp.int32))
    attended = attended.transpose(1, 2, 0, 3).reshape(TOKENS, H, DH)
    gate = jax.nn.sigmoid(gate_logits.astype(jnp.float32)).reshape(TOKENS, H, DH)
    return (gate * attended.astype(jnp.float32)).astype(jnp.bfloat16).reshape(TOKENS, H * DH)
```

```python
import jax
import jax.numpy as jnp
from jax import lax
from jax.experimental import pallas as pl
from jax.experimental.pallas import tpu as pltpu
from jax.sharding import Mesh
from jax.sharding import PartitionSpec as P

H = 32
KVH = 8
DH = 128
BLOCK = 64
NV = 16
NS = 8
ROWS = 32
LO = 16
HI = 32
GROUP = 4
LOWEST = -3.0e38
EXP2_SCALE = DH**-0.5 * 1.4426950408889634

VERT, QDYN, QNAT, KVNAT, IN_ROWS = 0, 64, 192, 256, 320
OV, OS, STATS, OUT_ROWS = 0, 128, 192, 224
SLOTS = GROUP + 2
L_LANE = 64
M_HEAD, M_SLOT, M_MASK, M_KV, M_HI, M_LO, M_LEN = 0, 32, 64, 96, 104, 105, 106

bf16 = jnp.bfloat16
f32 = jnp.float32
SMEM = pl.BlockSpec(memory_space=pltpu.SMEM)
VMEM = pl.BlockSpec(memory_space=pltpu.VMEM)


def tables(vertical_blocks, slash_offsets, slash_count):
    hi = lax.axis_index("hi")
    lo = lax.axis_index("lo")
    heads = jnp.arange(H, dtype=jnp.int32)
    groups = H // GROUP
    order = slash_count * H + heads
    rank = jnp.sum((order[None, :] < order[:, None]).astype(jnp.int32), axis=1)
    within = rank // groups
    place = rank % groups
    group = jnp.where(within % 2 == 0, place, groups - 1 - place)
    slot = group * GROUP + within
    head_of = jnp.sum(jnp.where(slot[None, :] == heads[:, None], heads[None, :], 0), axis=1)
    live = jnp.arange(NS, dtype=jnp.int32)[None, :] < slash_count[:, None]
    mask = jnp.sum(jnp.where(live, jnp.left_shift(1, slash_offsets), 0), axis=1)
    shard = hi * 2 + lo // (LO // 2)
    here = jnp.any(vertical_blocks // 4 == shard, axis=1)
    kv_of = jnp.sum(
        jnp.where(
            (group[None, :] == jnp.arange(groups, dtype=jnp.int32)[:, None]) & here[None, :],
            (heads // (H // KVH))[None, :],
            0,
        ),
        axis=1,
    )
    return jnp.concatenate([head_of, slot, mask, kv_of, jnp.stack([hi, lo])]).astype(jnp.int32)


def entry_kernel(meta, q_ref, kv_ref, out_ref):
    def q_cols(head):
        return q_ref[:, pl.ds(pl.multiple_of(head * DH, DH), DH)]

    def kv_cols(which, head):
        return kv_ref[:, pl.ds(pl.multiple_of(which * KVH * DH + head * DH, DH), DH)]

    for g in range(KVH):
        kv_head = meta[M_KV + g]
        parts = [kv_cols(0, kv_head), kv_cols(1, kv_head)]
        parts += [q_cols(meta[M_HEAD + g * GROUP + p]) for p in range(GROUP)]
        tail = [kv_cols(0, g), kv_cols(1, g)]
        for c in range(2):
            own = [q_cols(4 * g + 2 * c), q_cols(4 * g + 2 * c + 1)]
            for n, part in enumerate(parts + own + tail):
                out_ref[2 * g + c, n * ROWS : (n + 1) * ROWS, :] = part


def pick_kernel(meta, vert_ref, in_ref, spread_ref, kv_ref):
    lo = meta[M_LO]
    g = lo >> 1
    c = lo & 1
    shard = meta[M_HI] * 2 + c
    block = jnp.int32(0)
    for p in range(GROUP):
        head = meta[M_HEAD + g * GROUP + p]
        for j in range(NV):
            v = vert_ref[head, j]
            block = jnp.where((v >> 2) == shard, v & 3, block)
    first = c * (LO // 2) + 2 * block
    for half in range(2):
        for which in range(2):
            part = in_ref[first + half, VERT + which * ROWS : VERT + (which + 1) * ROWS, :]
            at = which * BLOCK + half * ROWS
            for d in range(HI):
                spread_ref[d, at : at + ROWS, :] = part
    kv_ref[...] = in_ref[:, KVNAT:, :]


def split(x, pieces):
    out = []
    for _ in range(pieces - 1):
        top = x.astype(bf16).astype(f32)
        out.append(top)
        x = x - top
    return out + [x]


def stats_tile(slot, row_max, row_sum, lane, base):
    for n, part in enumerate(split(row_max, 3)):
        base = jnp.where(lane == 3 * slot + n, part, base)
    for n, part in enumerate(split(row_sum, 2)):
        base = jnp.where(lane == L_LANE + 2 * slot + n, part, base)
    return base


def scores(q, k):
    return lax.dot_general(q, k, (((1,), (1,)), ((), ())), preferred_element_type=f32)


def slash_kernel(meta, in_ref, before_ref, out_ref, stats_ref, k_buf, v_buf):
    half = LO * ROWS
    k_buf[0:half, :] = before_ref[:, 0:ROWS, :].reshape(half, DH)
    v_buf[0:half, :] = before_ref[:, ROWS : 2 * ROWS, :].reshape(half, DH)
    k_buf[half:, :] = in_ref[:, KVNAT : KVNAT + ROWS, :].reshape(half, DH)
    v_buf[half:, :] = in_ref[:, KVNAT + ROWS : KVNAT + 2 * ROWS, :].reshape(half, DH)
    lo = meta[M_LO]
    first_block = meta[M_HI] * 8
    band = 8 * BLOCK
    offset = 8 - lax.broadcasted_iota(jnp.int32, (1, band), 1) // BLOCK
    causal = jnp.where(
        lax.broadcasted_iota(jnp.int32, (BLOCK, BLOCK), 1)
        <= lax.broadcasted_iota(jnp.int32, (BLOCK, BLOCK), 0),
        0.0,
        -jnp.inf,
    )
    lane = lax.broadcasted_iota(jnp.int32, (BLOCK, DH), 1)
    live = []
    for a in range(2):
        mask = meta[M_MASK + 2 * lo + a]
        live.append((jnp.right_shift(jnp.full((1, band), mask, jnp.int32), offset) & 1) == 1)
    for i in range(8):
        at = i * BLOCK
        reach = offset <= first_block + i
        q = jnp.concatenate(
            [
                in_ref[2 * i : 2 * i + 2, QNAT + a * ROWS : QNAT + (a + 1) * ROWS, :].reshape(
                    BLOCK, DH
                )
                for a in range(2)
            ],
            axis=0,
        )
        far = scores(q, k_buf[at : at + band, :])
        near = scores(q, k_buf[at + band : at + band + BLOCK, :])
        tile = jnp.zeros((BLOCK, DH), f32)
        for a in range(2):
            rows = slice(a * BLOCK, (a + 1) * BLOCK)
            s_far = far[rows] + jnp.where(live[a] & reach, 0.0, -jnp.inf)
            s_near = near[rows] + causal
            top = jnp.maximum(
                jnp.max(s_far, axis=1, keepdims=True), jnp.max(s_near, axis=1, keepdims=True)
            )
            e_far = jnp.exp2((s_far - top) * EXP2_SCALE)
            e_near = jnp.exp2((s_near - top) * EXP2_SCALE)
            total = jnp.sum(e_far, axis=1, keepdims=True) + jnp.sum(e_near, axis=1, keepdims=True)
            acc = jnp.dot(
                e_far.astype(bf16), v_buf[at : at + band, :], preferred_element_type=f32
            ) + jnp.dot(
                e_near.astype(bf16),
                v_buf[at + band : at + band + BLOCK, :],
                preferred_element_type=f32,
            )
            out_ref[2 * i : 2 * i + 2, a * ROWS : (a + 1) * ROWS, :] = acc.astype(bf16).reshape(
                2, ROWS, DH
            )
            tile = stats_tile(GROUP + a, top, total, lane, tile)
        stats_ref[2 * i : 2 * i + 2] = tile.astype(bf16).reshape(2, ROWS, DH)


def vertical_kernel(
    meta, vert_ref, in_ref, all_ref, slash_ref, slash_stats_ref, out_ref, k_buf, v_buf
):
    lo = meta[M_LO]
    g = lo >> 1
    c = lo & 1
    first_block = meta[M_HI] * 8
    width = NV * BLOCK
    out_ref[:, OS:STATS, :] = slash_ref[...]
    out_ref[:, STATS:, :] = slash_stats_ref[...]
    of_lane = lax.broadcasted_iota(jnp.int32, (1, width), 1) // BLOCK
    for p in range(GROUP):
        head = meta[M_HEAD + g * GROUP + p]
        count = jnp.int32(0)
        ids = jnp.full((1, width), 1 << 20, jnp.int32)
        for j in range(NV):
            k_buf[j * BLOCK : (j + 1) * BLOCK, :] = jnp.zeros((BLOCK, DH), bf16)
            v_buf[j * BLOCK : (j + 1) * BLOCK, :] = jnp.zeros((BLOCK, DH), bf16)
        for j in range(NV):
            v = vert_ref[head, j]
            mine = ((v >> 2) & 1) == c
            source = v >> 3
            at = pl.multiple_of(count * BLOCK, BLOCK)

            @pl.when(mine)
            def _():
                k_buf[pl.ds(at, BLOCK), :] = all_ref[source, 0:BLOCK, :]
                v_buf[pl.ds(at, BLOCK), :] = all_ref[source, BLOCK : 2 * BLOCK, :]

            ids = jnp.where(mine & (of_lane == count), v, ids)
            count = count + mine.astype(jnp.int32)
        mask = jnp.full((1, width), meta[M_MASK + head], jnp.int32)

        def attend(n):
            size = n * BLOCK
            k_all = k_buf[0:size, :]
            v_all = v_buf[0:size, :]
            lane = lax.broadcasted_iota(jnp.int32, (2 * BLOCK, DH), 1)
            for i in range(4):
                q = in_ref[
                    4 * i : 4 * i + 4, QDYN + p * ROWS : QDYN + (p + 1) * ROWS, :
                ].reshape(2 * BLOCK, DH)
                s = scores(q, k_all)
                parts = []
                for t in range(2):
                    distance = first_block + 2 * i + t - ids[:, 0:size]
                    slashed = jnp.right_shift(mask[:, 0:size], jnp.clip(distance, 0, 31)) & 1
                    bias = jnp.where((distance > 0) & (slashed == 0), 0.0, -jnp.inf)
                    parts.append(s[t * BLOCK : (t + 1) * BLOCK] + bias)
                s = jnp.concatenate(parts, axis=0)
                top = jnp.maximum(jnp.max(s, axis=1, keepdims=True), LOWEST)
                e = jnp.exp2((s - top) * EXP2_SCALE)
                total = jnp.sum(e, axis=1, keepdims=True)
                acc = jnp.dot(e.astype(bf16), v_all, preferred_element_type=f32)
                out_ref[4 * i : 4 * i + 4, OV + p * ROWS : OV + (p + 1) * ROWS, :] = acc.astype(
                    bf16
                ).reshape(4, ROWS, DH)
                base = out_ref[4 * i : 4 * i + 4, STATS:, :].reshape(2 * BLOCK, DH).astype(f32)
                tile = stats_tile(p, top, total, lane, base)
                out_ref[4 * i : 4 * i + 4, STATS:, :] = tile.astype(bf16).reshape(4, ROWS, DH)

        for low, n in ((0, 8), (8, 12), (12, 16)):

            @pl.when((count > low if low else count >= 0) & (count <= n))
            def _(n=n):
                attend(n)


def exit_kernel(meta, in_ref, gate_ref, out_ref, m_buf, l_buf):
    row = lax.broadcasted_iota(jnp.int32, (DH, SLOTS * DH), 0)
    col = lax.broadcasted_iota(jnp.int32, (DH, SLOTS * DH), 1) // DH
    m_pick = jnp.where((row >= 3 * col) & (row < 3 * col + 3), 1.0, 0.0).astype(bf16)
    l_at = row - L_LANE
    l_pick = jnp.where((l_at >= 2 * col) & (l_at < 2 * col + 2), 1.0, 0.0).astype(bf16)
    stats = in_ref[:, STATS:, :].reshape(LO * ROWS, DH)
    m_buf[...] = jnp.dot(stats, m_pick, preferred_element_type=f32).reshape(
        LO, ROWS, SLOTS * DH
    )
    l_buf[...] = jnp.dot(stats, l_pick, preferred_element_type=f32).reshape(
        LO, ROWS, SLOTS * DH
    )
    for h in range(H):
        source = h // 2
        a = h % 2
        cols = slice((GROUP + a) * DH, (GROUP + a + 1) * DH)
        tops = [m_buf[source, :, cols]]
        sums = [l_buf[source, :, cols]]
        accs = [in_ref[source, OS + a * ROWS : OS + (a + 1) * ROWS, :]]
        slot = meta[M_SLOT + h]
        p = slot & 3
        lanes = pl.ds(pl.multiple_of(p * DH, DH), DH)
        for c in range(2):
            source = 2 * (slot >> 2) + c
            tops.append(m_buf[source, :, lanes])
            sums.append(l_buf[source, :, lanes])
            accs.append(in_ref[source, pl.ds(pl.multiple_of(OV + p * ROWS, ROWS), ROWS), :])
        best = jnp.maximum(jnp.maximum(tops[0], tops[1]), tops[2])
        num = jnp.zeros((ROWS, DH), f32)
        den = jnp.zeros((ROWS, DH), f32)
        for top, total, acc in zip(tops, sums, accs):
            w = jnp.exp2((top - best) * EXP2_SCALE)
            num = num + w * acc.astype(f32)
            den = den + w * total
        attended = (num / den).astype(bf16).astype(f32)
        gate = gate_ref[:, h * DH : (h + 1) * DH].astype(f32)
        out_ref[:, h * DH : (h + 1) * DH] = (jax.nn.sigmoid(gate) * attended).astype(bf16)


def call(kernel, out_shape, in_specs, scratch=(), name=None):
    return pl.pallas_call(
        kernel,
        out_shape=out_shape,
        in_specs=in_specs,
        out_specs=jax.tree.map(lambda _: VMEM, out_shape),
        scratch_shapes=list(scratch),
        name=name,
    )


def body(queries, key_values, gate_logits, vertical_blocks, slash_offsets, slash_count):
    meta = tables(vertical_blocks, slash_offsets, slash_count)
    flat_kv = key_values.reshape(ROWS, 2 * KVH * DH)
    sent = call(
        entry_kernel,
        jax.ShapeDtypeStruct((LO, IN_ROWS, DH), bf16),
        [SMEM, VMEM, VMEM],
        name="entry",
    )(meta, queries, flat_kv)
    mine = lax.all_to_all(sent, "lo", 0, 0, tiled=True)
    spread, kv_own = call(
        pick_kernel,
        (
            jax.ShapeDtypeStruct((HI, 2 * BLOCK, DH), bf16),
            jax.ShapeDtypeStruct((LO, 2 * ROWS, DH), bf16),
        ),
        [SMEM, SMEM, VMEM],
        name="pick",
    )(meta, vertical_blocks, mine)
    verticals = lax.all_to_all(spread, "hi", 0, 0, tiled=True)
    kv_before = lax.ppermute(kv_own, "hi", [(i, i + 1) for i in range(HI - 1)])
    slash, slash_stats = call(
        slash_kernel,
        (
            jax.ShapeDtypeStruct((LO, 2 * ROWS, DH), bf16),
            jax.ShapeDtypeStruct((LO, ROWS, DH), bf16),
        ),
        [SMEM, VMEM, VMEM],
        [pltpu.VMEM((2 * LO * ROWS, DH), bf16)] * 2,
        name="slash",
    )(meta, mine, kv_before)
    partial = call(
        vertical_kernel,
        jax.ShapeDtypeStruct((LO, OUT_ROWS, DH), bf16),
        [SMEM, SMEM, VMEM, VMEM, VMEM, VMEM],
        [pltpu.VMEM((NV * BLOCK, DH), bf16)] * 2,
        name="vertical",
    )(meta, vertical_blocks, mine, verticals, slash, slash_stats)
    back = lax.all_to_all(partial, "lo", 0, 0, tiled=True)
    return call(
        exit_kernel,
        jax.ShapeDtypeStruct((ROWS, H * DH), bf16),
        [SMEM, VMEM, VMEM],
        [pltpu.VMEM((LO, ROWS, SLOTS * DH), f32)] * 2,
        name="exit",
    )(meta, back, gate_logits)


def solution(mesh):
    pairs = Mesh(mesh.devices.reshape(HI, LO), ("hi", "lo"))
    tokens = P(("hi", "lo"))
    return jax.shard_map(
        body,
        mesh=pairs,
        in_specs=(tokens, tokens, tokens, P(), P(), P()),
        out_specs=tokens,
        check_vma=False,
    )
```

```python
import jax
import jax.numpy as jnp
from jax import lax
from jax.experimental import pallas as pl
from jax.experimental.pallas import tpu as pltpu
from jax.sharding import Mesh
from jax.sharding import PartitionSpec as P

H = 32
KVH = 8
DH = 128
BLOCK = 64
NV = 16
NS = 8
ROWS = 32
LO = 16
NY = 8
NK = 4
HI = NY * NK
GROUP = 4
LOWEST = -3.0e38
EXP2_SCALE = DH**-0.5 * 1.4426950408889634

VERT, QDYN, KVNAT, QNAT, IN_ROWS = 0, 64, 128, 160, 224
OV, OS, STATS, OUT_ROWS = 0, 128, 192, 224
SLOTS = GROUP + 2
L_LANE = 8
PART = 32
M_HEAD, M_SLOT, M_MASK, M_KV, M_HI, M_LO, M_LEN = 0, 32, 64, 96, 104, 105, 106

bf16 = jnp.bfloat16
f32 = jnp.float32
SMEM = pl.BlockSpec(memory_space=pltpu.SMEM)
VMEM = pl.BlockSpec(memory_space=pltpu.VMEM)


def tables(vertical_blocks, slash_offsets, slash_count):
    hi = lax.axis_index(("y", "k"))
    lo = lax.axis_index("lo")
    heads = jnp.arange(H, dtype=jnp.int32)
    groups = H // GROUP
    order = slash_count * H + heads
    rank = jnp.sum((order[None, :] < order[:, None]).astype(jnp.int32), axis=1)
    within = rank // groups
    place = rank % groups
    group = jnp.where(within % 2 == 0, place, groups - 1 - place)
    slot = group * GROUP + within
    head_of = jnp.sum(jnp.where(slot[None, :] == heads[:, None], heads[None, :], 0), axis=1)
    live = jnp.arange(NS, dtype=jnp.int32)[None, :] < slash_count[:, None]
    mask = jnp.sum(jnp.where(live, jnp.left_shift(1, slash_offsets), 0), axis=1)
    shard = hi * 2 + lo // (LO // 2)
    here = jnp.any(vertical_blocks // 4 == shard, axis=1)
    kv_of = jnp.sum(
        jnp.where(
            (group[None, :] == jnp.arange(groups, dtype=jnp.int32)[:, None]) & here[None, :],
            (heads // (H // KVH))[None, :],
            0,
        ),
        axis=1,
    )
    return jnp.concatenate([head_of, slot, mask, kv_of, jnp.stack([hi, lo])]).astype(jnp.int32)


def entry_kernel(meta, q_ref, kv_ref, out_ref):
    def q_cols(head):
        return q_ref[:, pl.ds(pl.multiple_of(head * DH, DH), DH)]

    def kv_cols(which, head):
        return kv_ref[:, pl.ds(pl.multiple_of(which * KVH * DH + head * DH, DH), DH)]

    for g in range(KVH):
        kv_head = meta[M_KV + g]
        vert = [kv_cols(0, kv_head), kv_cols(1, kv_head)]
        for c in range(2):
            parts = vert + [q_cols(meta[M_HEAD + g * GROUP + 2 * c + p]) for p in range(2)]
            parts += [kv_cols(c, g), q_cols(4 * g + 2 * c), q_cols(4 * g + 2 * c + 1)]
            for n, part in enumerate(parts):
                out_ref[2 * g + c, n * ROWS : (n + 1) * ROWS, :] = part


def pick_kernel(meta, vert_ref, in_ref, spread_ref, swap_ref, kv_ref):
    lo = meta[M_LO]
    g = lo >> 1
    c = lo & 1
    shard = meta[M_HI] * 2 + c
    block = jnp.int32(0)
    for p in range(GROUP):
        head = meta[M_HEAD + g * GROUP + p]
        for j in range(NV):
            v = vert_ref[head, j]
            block = jnp.where((v >> 2) == shard, v & 3, block)
    first = c * (LO // 2) + 2 * block
    for half in range(2):
        for which in range(2):
            part = in_ref[first + half, VERT + which * ROWS : VERT + (which + 1) * ROWS, :]
            at = which * BLOCK + half * ROWS
            for d in range(NK):
                spread_ref[d, at : at + ROWS, :] = part
    swap_ref[...] = in_ref[:, QDYN:QNAT, :]
    kv_ref[...] = in_ref[:, KVNAT:QNAT, :]


def scores(q, k):
    return lax.dot_general(q, k, (((1,), (1,)), ((), ())), preferred_element_type=f32)


def slash_kernel(meta, in_ref, swap_ref, before_ref, before_swap_ref, out_ref, stats_ref, k_buf, v_buf):
    half = LO * ROWS
    lo = meta[M_LO]
    for c in range(2):

        @pl.when((lo & 1) == c)
        def _(c=c):
            mine, other = (k_buf, v_buf) if c == 0 else (v_buf, k_buf)
            mine[0:half, :] = before_ref[...].reshape(half, DH)
            other[0:half, :] = before_swap_ref[...].reshape(half, DH)
            mine[half:, :] = in_ref[:, KVNAT:QNAT, :].reshape(half, DH)
            other[half:, :] = swap_ref[:, KVNAT - QDYN :, :].reshape(half, DH)

    first_block = meta[M_HI] * 8
    band = 8 * BLOCK
    offset = 8 - lax.broadcasted_iota(jnp.int32, (1, band), 1) // BLOCK
    causal = jnp.where(
        lax.broadcasted_iota(jnp.int32, (BLOCK, BLOCK), 1)
        <= lax.broadcasted_iota(jnp.int32, (BLOCK, BLOCK), 0),
        0.0,
        -jnp.inf,
    )
    lane = lax.broadcasted_iota(jnp.int32, (BLOCK, DH), 1)
    live = []
    for a in range(2):
        mask = meta[M_MASK + 2 * lo + a]
        live.append((jnp.right_shift(jnp.full((1, band), mask, jnp.int32), offset) & 1) == 1)

    def step(i, _):
        at = pl.multiple_of(i * BLOCK, BLOCK)
        near_at = pl.multiple_of(i * BLOCK + band, BLOCK)
        reach = offset <= first_block + i
        two = pl.ds(2 * i, 2)
        q = jnp.concatenate(
            [
                in_ref[two, QNAT + a * ROWS : QNAT + (a + 1) * ROWS, :].reshape(BLOCK, DH)
                for a in range(2)
            ],
            axis=0,
        )
        far = scores(q, k_buf[pl.ds(at, band), :])
        near = scores(q, k_buf[pl.ds(near_at, BLOCK), :])
        tile = jnp.zeros((BLOCK, DH), f32)
        for a in range(2):
            rows = slice(a * BLOCK, (a + 1) * BLOCK)
            s_far = far[rows] + jnp.where(live[a] & reach, 0.0, -jnp.inf)
            s_near = near[rows] + causal
            top = jnp.maximum(
                jnp.max(s_far, axis=1, keepdims=True), jnp.max(s_near, axis=1, keepdims=True)
            )
            e_far = jnp.exp2((s_far - top) * EXP2_SCALE)
            e_near = jnp.exp2((s_near - top) * EXP2_SCALE)
            total = jnp.sum(e_far, axis=1, keepdims=True) + jnp.sum(e_near, axis=1, keepdims=True)
            acc = jnp.dot(
                e_far.astype(bf16), v_buf[pl.ds(at, band), :], preferred_element_type=f32
            ) + jnp.dot(
                e_near.astype(bf16), v_buf[pl.ds(near_at, BLOCK), :], preferred_element_type=f32
            )
            out_ref[two, a * ROWS : (a + 1) * ROWS, :] = acc.astype(bf16).reshape(2, ROWS, DH)
            tile = jnp.where(lane == GROUP + a, top, tile)
            tile = jnp.where(lane == L_LANE + GROUP + a, total, tile)
        stats_ref[two] = tile.reshape(2, ROWS, DH)
        return 0

    lax.fori_loop(0, 8, step, 0)


def vertical_kernel(
    meta,
    vert_ref,
    in_ref,
    swap_ref,
    all_ref,
    slash_ref,
    slash_stats_ref,
    out_ref,
    q_buf,
    k_buf,
    v_buf,
    stats_buf,
):
    lo = meta[M_LO]
    g = lo >> 1
    c = lo & 1
    first_block = meta[M_HI] * 8
    tokens = LO * ROWS
    width = NV * BLOCK
    out_ref[:, OS:STATS, :] = slash_ref[...]
    stats_buf[...] = slash_stats_ref[...].reshape(tokens, DH)
    k_buf[...] = jnp.zeros(k_buf.shape, bf16)
    v_buf[...] = jnp.zeros(v_buf.shape, bf16)
    for t in range(2):
        rows = slice(t * ROWS, (t + 1) * ROWS)
        q_buf[2 * c + t] = in_ref[:, QDYN + t * ROWS : QDYN + (t + 1) * ROWS, :].reshape(tokens, DH)
        q_buf[2 * (1 - c) + t] = swap_ref[:, rows, :].reshape(tokens, DH)
    of_lane = lax.broadcasted_iota(jnp.int32, (1, width), 1) // BLOCK
    lane = lax.broadcasted_iota(jnp.int32, (2 * BLOCK, DH), 1)

    def head_step(p, _):
        head = meta[M_HEAD + g * GROUP + p]
        count = jnp.int32(0)
        ids = jnp.full((1, width), 1 << 20, jnp.int32)
        for j in range(NV):
            v = vert_ref[head, j]
            mine = ((v >> 2) & 1) == c
            source = v >> 3
            at = pl.multiple_of(count * BLOCK, BLOCK)
            k_buf[pl.ds(at, BLOCK), :] = all_ref[source, 0:BLOCK, :]
            v_buf[pl.ds(at, BLOCK), :] = all_ref[source, BLOCK : 2 * BLOCK, :]
            ids = jnp.where(of_lane == jnp.where(mine, count, NV), v, ids)
            count = count + mine.astype(jnp.int32)
        mask = jnp.full((1, width), meta[M_MASK + head], jnp.int32)

        def attend(n):
            size = n * BLOCK

            def step(i, _):
                at = pl.multiple_of(i * 2 * BLOCK, 2 * BLOCK)
                s = scores(q_buf[p, pl.ds(at, 2 * BLOCK), :], k_buf[0:size, :])
                parts = []
                for t in range(2):
                    distance = first_block + 2 * i + t - ids[:, 0:size]
                    slashed = jnp.right_shift(mask[:, 0:size], jnp.clip(distance, 0, 31)) & 1
                    bias = jnp.where((distance > 0) & (slashed == 0), 0.0, -jnp.inf)
                    parts.append(s[t * BLOCK : (t + 1) * BLOCK] + bias)
                s = jnp.concatenate(parts, axis=0)
                top = jnp.maximum(jnp.max(s, axis=1, keepdims=True), LOWEST)
                e = jnp.exp2((s - top) * EXP2_SCALE)
                total = jnp.sum(e, axis=1, keepdims=True)
                acc = jnp.dot(e.astype(bf16), v_buf[0:size, :], preferred_element_type=f32)
                rows = pl.ds(pl.multiple_of(OV + p * ROWS, ROWS), ROWS)
                out_ref[pl.ds(4 * i, 4), rows, :] = acc.astype(bf16).reshape(4, ROWS, DH)
                tile = stats_buf[pl.ds(at, 2 * BLOCK), :]
                tile = jnp.where(lane == p, top, tile)
                stats_buf[pl.ds(at, 2 * BLOCK), :] = jnp.where(lane == L_LANE + p, total, tile)
                return 0

            lax.fori_loop(0, 4, step, 0)

        for low, n in ((-1, 8), (8, 12), (12, 16)):

            @pl.when((count > low) & (count <= n))
            def _(n=n):
                attend(n)

        return 0

    lax.fori_loop(0, GROUP, head_step, 0)
    stats = stats_buf[...]
    first = stats.astype(bf16).astype(f32)
    stats = stats - first
    second = stats.astype(bf16).astype(f32)
    third = stats - second
    packed = first + pltpu.roll(second, PART, 1) + pltpu.roll(third, 2 * PART, 1)
    out_ref[:, STATS:, :] = packed.astype(bf16).reshape(LO, ROWS, DH)


def exit_kernel(meta, in_ref, gate_ref, out_ref, m_buf, l_buf):
    row = lax.broadcasted_iota(jnp.int32, (DH, SLOTS * DH), 0)
    col = lax.broadcasted_iota(jnp.int32, (DH, SLOTS * DH), 1) // DH
    row = jnp.where(row < 3 * PART, row % PART, PART)
    m_pick = jnp.where(row == col, 1.0, 0.0).astype(bf16)
    l_pick = jnp.where(row == col + L_LANE, 1.0, 0.0).astype(bf16)
    stats = in_ref[:, STATS:, :].reshape(LO * ROWS, DH)
    m_buf[...] = jnp.dot(stats, m_pick, preferred_element_type=f32).reshape(LO, ROWS, SLOTS * DH)
    l_buf[...] = jnp.dot(stats, l_pick, preferred_element_type=f32).reshape(LO, ROWS, SLOTS * DH)

    def source_step(n, _):
        for a in range(2):
            h = 2 * n + a
            cols = slice((GROUP + a) * DH, (GROUP + a + 1) * DH)
            tops = [m_buf[n, :, cols]]
            sums = [l_buf[n, :, cols]]
            accs = [in_ref[n, OS + a * ROWS : OS + (a + 1) * ROWS, :]]
            slot = meta[M_SLOT + h]
            p = slot & 3
            lanes = pl.ds(pl.multiple_of(p * DH, DH), DH)
            for c in range(2):
                source = 2 * (slot >> 2) + c
                tops.append(m_buf[source, :, lanes])
                sums.append(l_buf[source, :, lanes])
                accs.append(in_ref[source, pl.ds(pl.multiple_of(OV + p * ROWS, ROWS), ROWS), :])
            best = jnp.maximum(jnp.maximum(tops[0], tops[1]), tops[2])
            num = jnp.zeros((ROWS, DH), f32)
            den = jnp.zeros((ROWS, DH), f32)
            for top, total, acc in zip(tops, sums, accs):
                w = jnp.exp2((top - best) * EXP2_SCALE)
                num = num + w * acc.astype(f32)
                den = den + w * total
            attended = (num / den).astype(bf16).astype(f32)
            at = pl.ds(pl.multiple_of(h * DH, DH), DH)
            gate = gate_ref[:, at].astype(f32)
            out_ref[:, at] = (jax.nn.sigmoid(gate) * attended).astype(bf16)
        return 0

    lax.fori_loop(0, LO, source_step, 0, unroll=2)


def call(kernel, out_shape, in_specs, scratch=(), name=None):
    return pl.pallas_call(
        kernel,
        out_shape=out_shape,
        in_specs=in_specs,
        out_specs=jax.tree.map(lambda _: VMEM, out_shape),
        scratch_shapes=list(scratch),
        name=name,
    )


def shape(rows, dtype=bf16, lead=LO):
    return jax.ShapeDtypeStruct((lead, rows, DH), dtype)


def body(queries, key_values, gate_logits, vertical_blocks, slash_offsets, slash_count):
    meta = tables(vertical_blocks, slash_offsets, slash_count)
    flat_kv = key_values.reshape(ROWS, 2 * KVH * DH)
    sent = call(entry_kernel, shape(IN_ROWS), [SMEM, VMEM, VMEM], name="entry")(
        meta, queries, flat_kv
    )
    mine = lax.all_to_all(sent, "lo", 0, 0, tiled=True)
    spread, swap, kv_own = call(
        pick_kernel,
        (shape(2 * BLOCK, lead=NK), shape(QNAT - QDYN), shape(ROWS)),
        [SMEM, SMEM, VMEM],
        name="pick",
    )(meta, vertical_blocks, mine)
    row = lax.all_to_all(spread, "k", 0, 0, tiled=True).reshape(1, NK * 2 * BLOCK, DH)
    spread_row = jnp.broadcast_to(row, (NY, NK * 2 * BLOCK, DH))
    verticals = lax.all_to_all(spread_row, "y", 0, 0, tiled=True).reshape(HI, 2 * BLOCK, DH)
    partner = [(i, i ^ 1) for i in range(LO)]
    swapped = lax.ppermute(swap, "lo", partner)
    before = lax.ppermute(kv_own, ("y", "k"), [(i, i + 1) for i in range(HI - 1)])
    before_swap = lax.ppermute(before, "lo", partner)
    slash, slash_stats = call(
        slash_kernel,
        (shape(2 * ROWS), shape(ROWS, f32)),
        [SMEM, VMEM, VMEM, VMEM, VMEM],
        [pltpu.VMEM((2 * LO * ROWS, DH), bf16)] * 2,
        name="slash",
    )(meta, mine, swapped, before, before_swap)
    partial = call(
        vertical_kernel,
        shape(OUT_ROWS),
        [SMEM, SMEM, VMEM, VMEM, VMEM, VMEM, VMEM],
        [
            pltpu.VMEM((GROUP, LO * ROWS, DH), bf16),
            pltpu.VMEM(((NV + 1) * BLOCK, DH), bf16),
            pltpu.VMEM(((NV + 1) * BLOCK, DH), bf16),
            pltpu.VMEM((LO * ROWS, DH), f32),
        ],
        name="vertical",
    )(meta, vertical_blocks, mine, swapped, verticals, slash, slash_stats)
    back = lax.all_to_all(partial, "lo", 0, 0, tiled=True)
    return call(
        exit_kernel,
        jax.ShapeDtypeStruct((ROWS, H * DH), bf16),
        [SMEM, VMEM, VMEM],
        [pltpu.VMEM((LO, ROWS, SLOTS * DH), f32)] * 2,
        name="exit",
    )(meta, back, gate_logits)


def solution(mesh):
    pairs = Mesh(mesh.devices.reshape(NY, NK, LO), ("y", "k", "lo"))
    tokens = P(("y", "k", "lo"))
    return jax.shard_map(
        body,
        mesh=pairs,
        in_specs=(tokens, tokens, tokens, P(), P(), P()),
        out_specs=tokens,
        check_vma=False,
    )
```

```python
import jax
import jax.numpy as jnp
from jax import lax
from jax.experimental import pallas as pl
from jax.experimental.pallas import tpu as pltpu
from jax.sharding import Mesh
from jax.sharding import PartitionSpec as P

H = 32
KVH = 8
DH = 128
BLOCK = 64
NV = 16
NS = 8
ROWS = 32
LO = 16
NY = 8
NK = 4
HI = NY * NK
GROUP = 4
LOWEST = -3.0e38
EXP2_SCALE = DH**-0.5 * 1.4426950408889634

VERT, QDYN, KVNAT, QNAT, IN_ROWS = 0, 64, 128, 160, 224
OV, OS, STATS, OUT_ROWS = 0, 128, 192, 224
SLOTS = GROUP + 2
L_LANE = 8
PART = 32
M_HEAD, M_SLOT, M_MASK, M_KV, M_HI, M_LO, M_LEN = 0, 32, 64, 96, 104, 105, 106

bf16 = jnp.bfloat16
f32 = jnp.float32
SMEM = pl.BlockSpec(memory_space=pltpu.SMEM)
VMEM = pl.BlockSpec(memory_space=pltpu.VMEM)
LOADED = pl.BlockSpec(memory_space=pltpu.VMEM)


def tables(vertical_blocks, slash_offsets, slash_count):
    hi = lax.axis_index(("y", "k"))
    lo = lax.axis_index("lo")
    heads = jnp.arange(H, dtype=jnp.int32)
    groups = H // GROUP
    order = slash_count * H + heads
    rank = jnp.sum((order[None, :] < order[:, None]).astype(jnp.int32), axis=1)
    within = rank // groups
    place = rank % groups
    group = jnp.where(within % 2 == 0, place, groups - 1 - place)
    slot = group * GROUP + within
    head_of = jnp.sum(jnp.where(slot[None, :] == heads[:, None], heads[None, :], 0), axis=1)
    live = jnp.arange(NS, dtype=jnp.int32)[None, :] < slash_count[:, None]
    mask = jnp.sum(jnp.where(live, jnp.left_shift(1, slash_offsets), 0), axis=1)
    shard = hi * 2 + lo // (LO // 2)
    here = jnp.any(vertical_blocks // 4 == shard, axis=1)
    kv_of = jnp.sum(
        jnp.where(
            (group[None, :] == jnp.arange(groups, dtype=jnp.int32)[:, None]) & here[None, :],
            (heads // (H // KVH))[None, :],
            0,
        ),
        axis=1,
    )
    return jnp.concatenate([head_of, slot, mask, kv_of, jnp.stack([hi, lo])]).astype(jnp.int32)


def entry_kernel(meta, q_ref, kv_ref, out_ref):
    def q_cols(head):
        return q_ref[:, pl.ds(pl.multiple_of(head * DH, DH), DH)]

    def kv_cols(which, head):
        return kv_ref[:, pl.ds(pl.multiple_of(which * KVH * DH + head * DH, DH), DH)]

    for g in range(KVH):
        kv_head = meta[M_KV + g]
        vert = [kv_cols(0, kv_head), kv_cols(1, kv_head)]
        for c in range(2):
            parts = vert + [q_cols(meta[M_HEAD + g * GROUP + 2 * c + p]) for p in range(2)]
            parts += [kv_cols(c, g), q_cols(4 * g + 2 * c), q_cols(4 * g + 2 * c + 1)]
            for n, part in enumerate(parts):
                out_ref[2 * g + c, n * ROWS : (n + 1) * ROWS, :] = part


def pick_kernel(meta, vert_ref, in_ref, spread_ref, swap_ref, kv_ref):
    lo = meta[M_LO]
    g = lo >> 1
    c = lo & 1
    shard = meta[M_HI] * 2 + c
    block = jnp.int32(0)
    for p in range(GROUP):
        head = meta[M_HEAD + g * GROUP + p]
        for j in range(NV):
            v = vert_ref[head, j]
            block = jnp.where((v >> 2) == shard, v & 3, block)
    first = c * (LO // 2) + 2 * block
    for half in range(2):
        for which in range(2):
            part = in_ref[first + half, VERT + which * ROWS : VERT + (which + 1) * ROWS, :]
            at = which * BLOCK + half * ROWS
            for d in range(NK):
                spread_ref[d, at : at + ROWS, :] = part
    swap_ref[...] = in_ref[:, QDYN:QNAT, :]
    kv_ref[...] = in_ref[:, KVNAT:QNAT, :]


def scores(q, k):
    return lax.dot_general(q, k, (((1,), (1,)), ((), ())), preferred_element_type=f32)


def slash_kernel(
    meta, in_ref, swap_ref, before_ref, before_swap_ref, out_ref, stats_ref, q_ref, k_buf, v_buf
):
    half = LO * ROWS
    lo = meta[M_LO]
    core = lo & 1
    for t in range(2):
        rows = slice(t * ROWS, (t + 1) * ROWS)
        q_ref[2 * core + t] = in_ref[:, QDYN + t * ROWS : QDYN + (t + 1) * ROWS, :].reshape(half, DH)
        q_ref[2 * (1 - core) + t] = swap_ref[:, rows, :].reshape(half, DH)
    for c in range(2):

        @pl.when((lo & 1) == c)
        def _(c=c):
            mine, other = (k_buf, v_buf) if c == 0 else (v_buf, k_buf)
            mine[0:half, :] = before_ref[...].reshape(half, DH)
            other[0:half, :] = before_swap_ref[...].reshape(half, DH)
            mine[half:, :] = in_ref[:, KVNAT:QNAT, :].reshape(half, DH)
            other[half:, :] = swap_ref[:, KVNAT - QDYN :, :].reshape(half, DH)

    first_block = meta[M_HI] * 8
    band = 8 * BLOCK
    offset = 8 - lax.broadcasted_iota(jnp.int32, (1, band), 1) // BLOCK
    causal = jnp.where(
        lax.broadcasted_iota(jnp.int32, (BLOCK, BLOCK), 1)
        <= lax.broadcasted_iota(jnp.int32, (BLOCK, BLOCK), 0),
        0.0,
        -jnp.inf,
    )
    lane = lax.broadcasted_iota(jnp.int32, (BLOCK, DH), 1)
    live = []
    for a in range(2):
        mask = meta[M_MASK + 2 * lo + a]
        live.append((jnp.right_shift(jnp.full((1, band), mask, jnp.int32), offset) & 1) == 1)

    def step(i, _):
        at = pl.multiple_of(i * BLOCK, BLOCK)
        near_at = pl.multiple_of(i * BLOCK + band, BLOCK)
        reach = offset <= first_block + i
        two = pl.ds(2 * i, 2)
        q = jnp.concatenate(
            [
                in_ref[two, QNAT + a * ROWS : QNAT + (a + 1) * ROWS, :].reshape(BLOCK, DH)
                for a in range(2)
            ],
            axis=0,
        )
        far = scores(q, k_buf[pl.ds(at, band), :])
        near = scores(q, k_buf[pl.ds(near_at, BLOCK), :])
        tile = jnp.zeros((BLOCK, DH), f32)
        for a in range(2):
            rows = slice(a * BLOCK, (a + 1) * BLOCK)
            s_far = far[rows] + jnp.where(live[a] & reach, 0.0, -jnp.inf)
            s_near = near[rows] + causal
            top = jnp.maximum(
                jnp.max(s_far, axis=1, keepdims=True), jnp.max(s_near, axis=1, keepdims=True)
            )
            e_far = jnp.exp2((s_far - top) * EXP2_SCALE)
            e_near = jnp.exp2((s_near - top) * EXP2_SCALE)
            total = jnp.sum(e_far, axis=1, keepdims=True) + jnp.sum(e_near, axis=1, keepdims=True)
            acc = jnp.dot(
                e_far.astype(bf16), v_buf[pl.ds(at, band), :], preferred_element_type=f32
            ) + jnp.dot(
                e_near.astype(bf16), v_buf[pl.ds(near_at, BLOCK), :], preferred_element_type=f32
            )
            out_ref[two, a * ROWS : (a + 1) * ROWS, :] = acc.astype(bf16).reshape(2, ROWS, DH)
            tile = jnp.where(lane == GROUP + a, top, tile)
            tile = jnp.where(lane == L_LANE + GROUP + a, total, tile)
        stats_ref[two] = tile.reshape(2, ROWS, DH)
        return 0

    lax.fori_loop(0, 8, step, 0)


def vertical_kernel(
    meta,
    vert_ref,
    q_buf,
    all_ref,
    slash_ref,
    slash_stats_ref,
    out_ref,
    k_buf,
    v_buf,
    stats_buf,
):
    lo = meta[M_LO]
    g = lo >> 1
    c = lo & 1
    first_block = meta[M_HI] * 8
    tokens = LO * ROWS
    width = NV * BLOCK
    out_ref[:, OS:STATS, :] = slash_ref[...]
    stats_buf[...] = slash_stats_ref[...].reshape(tokens, DH)
    k_buf[...] = jnp.zeros(k_buf.shape, bf16)
    v_buf[...] = jnp.zeros(v_buf.shape, bf16)
    of_lane = lax.broadcasted_iota(jnp.int32, (1, width), 1) // BLOCK
    lane = lax.broadcasted_iota(jnp.int32, (2 * BLOCK, DH), 1)

    def head_step(p, _):
        head = meta[M_HEAD + g * GROUP + p]
        count = jnp.int32(0)
        ids = jnp.full((1, width), 1 << 20, jnp.int32)
        for j in range(NV):
            v = vert_ref[head, j]
            mine = ((v >> 2) & 1) == c
            source = v >> 3
            at = pl.multiple_of(count * BLOCK, BLOCK)
            k_buf[pl.ds(at, BLOCK), :] = all_ref[source, 0:BLOCK, :]
            v_buf[pl.ds(at, BLOCK), :] = all_ref[source, BLOCK : 2 * BLOCK, :]
            ids = jnp.where(of_lane == jnp.where(mine, count, NV), v, ids)
            count = count + mine.astype(jnp.int32)
        mask = jnp.full((1, width), meta[M_MASK + head], jnp.int32)

        def attend(n):
            size = n * BLOCK

            def step(i, _):
                at = pl.multiple_of(i * 2 * BLOCK, 2 * BLOCK)
                s = scores(q_buf[p, pl.ds(at, 2 * BLOCK), :], k_buf[0:size, :])
                parts = []
                for t in range(2):
                    distance = first_block + 2 * i + t - ids[:, 0:size]
                    slashed = jnp.right_shift(mask[:, 0:size], jnp.clip(distance, 0, 31)) & 1
                    bias = jnp.where((distance > 0) & (slashed == 0), 0.0, -jnp.inf)
                    parts.append(s[t * BLOCK : (t + 1) * BLOCK] + bias)
                s = jnp.concatenate(parts, axis=0)
                top = jnp.maximum(jnp.max(s, axis=1, keepdims=True), LOWEST)
                e = jnp.exp2((s - top) * EXP2_SCALE)
                total = jnp.sum(e, axis=1, keepdims=True)
                acc = jnp.dot(e.astype(bf16), v_buf[0:size, :], preferred_element_type=f32)
                rows = pl.ds(pl.multiple_of(OV + p * ROWS, ROWS), ROWS)
                out_ref[pl.ds(4 * i, 4), rows, :] = acc.astype(bf16).reshape(4, ROWS, DH)
                tile = stats_buf[pl.ds(at, 2 * BLOCK), :]
                tile = jnp.where(lane == p, top, tile)
                stats_buf[pl.ds(at, 2 * BLOCK), :] = jnp.where(lane == L_LANE + p, total, tile)
                return 0

            lax.fori_loop(0, 4, step, 0)

        for low, n in ((-1, 8), (8, 12), (12, 16)):

            @pl.when((count > low) & (count <= n))
            def _(n=n):
                attend(n)

        return 0

    lax.fori_loop(0, GROUP, head_step, 0)
    stats = stats_buf[...]
    first = stats.astype(bf16).astype(f32)
    stats = stats - first
    second = stats.astype(bf16).astype(f32)
    third = stats - second
    packed = first + pltpu.roll(second, PART, 1) + pltpu.roll(third, 2 * PART, 1)
    out_ref[:, STATS:, :] = packed.astype(bf16).reshape(LO, ROWS, DH)


def exit_kernel(meta, in_ref, gate_ref, out_ref, m_buf, l_buf):
    row = lax.broadcasted_iota(jnp.int32, (DH, SLOTS * DH), 0)
    col = lax.broadcasted_iota(jnp.int32, (DH, SLOTS * DH), 1) // DH
    row = jnp.where(row < 3 * PART, row % PART, PART)
    m_pick = jnp.where(row == col, 1.0, 0.0).astype(bf16)
    l_pick = jnp.where(row == col + L_LANE, 1.0, 0.0).astype(bf16)
    stats = in_ref[:, STATS:, :].reshape(LO * ROWS, DH)
    m_buf[...] = jnp.dot(stats, m_pick, preferred_element_type=f32).reshape(LO, ROWS, SLOTS * DH)
    l_buf[...] = jnp.dot(stats, l_pick, preferred_element_type=f32).reshape(LO, ROWS, SLOTS * DH)

    def source_step(n, _):
        for a in range(2):
            h = 2 * n + a
            cols = slice((GROUP + a) * DH, (GROUP + a + 1) * DH)
            tops = [m_buf[n, :, cols]]
            sums = [l_buf[n, :, cols]]
            accs = [in_ref[n, OS + a * ROWS : OS + (a + 1) * ROWS, :]]
            slot = meta[M_SLOT + h]
            p = slot & 3
            lanes = pl.ds(pl.multiple_of(p * DH, DH), DH)
            for c in range(2):
                source = 2 * (slot >> 2) + c
                tops.append(m_buf[source, :, lanes])
                sums.append(l_buf[source, :, lanes])
                accs.append(in_ref[source, pl.ds(pl.multiple_of(OV + p * ROWS, ROWS), ROWS), :])
            best = jnp.maximum(jnp.maximum(tops[0], tops[1]), tops[2])
            num = jnp.zeros((ROWS, DH), f32)
            den = jnp.zeros((ROWS, DH), f32)
            for top, total, acc in zip(tops, sums, accs):
                w = jnp.exp2((top - best) * EXP2_SCALE)
                num = num + w * acc.astype(f32)
                den = den + w * total
            attended = (num / den).astype(bf16).astype(f32)
            at = pl.ds(pl.multiple_of(h * DH, DH), DH)
            gate = gate_ref[:, at].astype(f32)
            out_ref[:, at] = (jax.nn.sigmoid(gate) * attended).astype(bf16)
        return 0

    lax.fori_loop(0, LO, source_step, 0, unroll=2)


def call(kernel, out_shape, in_specs, scratch=(), name=None, **options):
    run = pl.pallas_call(
        kernel,
        out_shape=out_shape,
        in_specs=in_specs,
        out_specs=tuple(VMEM for _ in out_shape) if isinstance(out_shape, tuple) else VMEM,
        scratch_shapes=list(scratch),
        name=name,
        **options,
    )

    def placed(*args):
        return run(
            *(
                pltpu.with_memory_space_constraint(arg, pltpu.VMEM) if spec is VMEM else arg
                for arg, spec in zip(args, in_specs)
            )
        )

    return placed


def shape(rows, dtype=bf16, lead=LO):
    return jax.ShapeDtypeStruct((lead, rows, DH), dtype)


def in_vmem(rows, lead=LO):
    return pltpu.VMEM((lead, rows, DH), bf16)


def body(queries, key_values, gate_logits, vertical_blocks, slash_offsets, slash_count):
    meta = tables(vertical_blocks, slash_offsets, slash_count)
    flat_kv = key_values.reshape(ROWS, 2 * KVH * DH)
    sent = call(entry_kernel, shape(IN_ROWS), [SMEM, VMEM, VMEM], name="entry")(
        meta, queries, flat_kv
    )
    mine = lax.all_to_all(sent, "lo", 0, 0, tiled=True)
    spread, swap, kv_own = call(
        pick_kernel,
        (shape(2 * BLOCK, lead=NK), in_vmem(QNAT - QDYN), in_vmem(ROWS)),
        [SMEM, SMEM, VMEM],
        name="pick",
    )(meta, vertical_blocks, mine)
    row = lax.all_to_all(spread, "k", 0, 0, tiled=True).reshape(1, NK * 2 * BLOCK, DH)
    before = lax.ppermute(kv_own, ("y", "k"), [(i, i + 1) for i in range(HI - 1)])
    row, before = lax.optimization_barrier((row, before))
    spread_row = jnp.broadcast_to(row, (NY, NK * 2 * BLOCK, DH))
    verticals = lax.all_to_all(spread_row, "y", 0, 0, tiled=True).reshape(HI, 2 * BLOCK, DH)
    partner = [(i, i ^ 1) for i in range(LO)]
    swapped = lax.ppermute(swap, "lo", partner)
    before_swap = lax.ppermute(before, "lo", partner)
    slash, slash_stats, vertical_queries = call(
        slash_kernel,
        (shape(2 * ROWS), shape(ROWS, f32), shape(LO * ROWS, lead=GROUP)),
        [SMEM, VMEM, VMEM, VMEM, VMEM],
        [pltpu.VMEM((2 * LO * ROWS, DH), bf16)] * 2,
        name="slash",
    )(meta, mine, swapped, before, before_swap)
    partial = call(
        vertical_kernel,
        shape(OUT_ROWS),
        [SMEM, SMEM, LOADED, VMEM, LOADED, LOADED],
        [
            pltpu.VMEM(((NV + 1) * BLOCK, DH), bf16),
            pltpu.VMEM(((NV + 1) * BLOCK, DH), bf16),
            pltpu.VMEM((LO * ROWS, DH), f32),
        ],
        name="vertical",
    )(meta, vertical_blocks, vertical_queries, verticals, slash, slash_stats)
    back = lax.all_to_all(partial, "lo", 0, 0, tiled=True)
    return call(
        exit_kernel,
        jax.ShapeDtypeStruct((ROWS, H * DH), bf16),
        [SMEM, VMEM, VMEM],
        [pltpu.VMEM((LO, ROWS, SLOTS * DH), f32)] * 2,
        name="exit",
    )(meta, back, gate_logits)


def solution(mesh):
    pairs = Mesh(mesh.devices.reshape(NY, NK, LO), ("y", "k", "lo"))
    tokens = P(("y", "k", "lo"))
    return jax.shard_map(
        body,
        mesh=pairs,
        in_specs=(tokens, tokens, tokens, P(), P(), P()),
        out_specs=tokens,
        check_vma=False,
    )
```

```python
import jax
import jax.numpy as jnp
from jax import lax
from jax.experimental import pallas as pl
from jax.experimental.pallas import tpu as pltpu
from jax.sharding import Mesh
from jax.sharding import PartitionSpec as P

H = 32
KVH = 8
DH = 128
BLOCK = 64
NV = 16
NS = 8
ROWS = 32
LO = 16
NY = 8
NK = 4
HI = NY * NK
GROUP = 4
LOWEST = -3.0e38
STEPS = 2
EXP2_SCALE = DH**-0.5 * 1.4426950408889634

VERT, QDYN, KVNAT, QNAT, IN_ROWS = 0, 64, 128, 160, 224
OV, OS, STATS, OUT_ROWS = 0, 128, 192, 224
SLOTS = GROUP + 2
L_LANE = 8
PART = 32
M_HEAD, M_SLOT, M_MASK, M_HI, M_LO = 0, 32, 64, 96, 97
E_HEAD, E_KV = 0, 32

bf16 = jnp.bfloat16
f32 = jnp.float32
SMEM = pl.BlockSpec(memory_space=pltpu.SMEM)
VMEM = pl.BlockSpec(memory_space=pltpu.VMEM)
LOADED = pl.BlockSpec(memory_space=pltpu.VMEM)


def tables(vertical_blocks, slash_offsets, slash_count):
    hi = lax.axis_index(("y", "k"))
    lo = lax.axis_index("lo")
    heads = jnp.arange(H, dtype=jnp.int32)
    groups = H // GROUP
    order = slash_count * H + heads
    rank = jnp.sum((order[None, :] < order[:, None]).astype(jnp.int32), axis=1)
    within = rank // groups
    place = rank % groups
    group = jnp.where(within % 2 == 0, place, groups - 1 - place)
    slot = group * GROUP + within
    head_of = jnp.sum(jnp.where(slot[None, :] == heads[:, None], heads[None, :], 0), axis=1)
    live = jnp.arange(NS, dtype=jnp.int32)[None, :] < slash_count[:, None]
    mask = jnp.sum(jnp.where(live, jnp.left_shift(1, slash_offsets), 0), axis=1)
    shard = hi * 2 + lo // (LO // 2)
    here = jnp.any(vertical_blocks // 4 == shard, axis=1)
    kv_of = jnp.sum(
        jnp.where(
            (group[None, :] == jnp.arange(groups, dtype=jnp.int32)[:, None]) & here[None, :],
            (heads // (H // KVH))[None, :],
            0,
        ),
        axis=1,
    )
    entry = jnp.concatenate([head_of, kv_of]).astype(jnp.int32)
    return entry, jnp.concatenate([head_of, slot, mask, jnp.stack([hi, lo])]).astype(jnp.int32)


def entry_kernel(meta, q_ref, kv_ref, out_ref):
    def q_cols(head):
        return q_ref[:, pl.ds(pl.multiple_of(head * DH, DH), DH)]

    def kv_cols(which, head):
        return kv_ref[:, pl.ds(pl.multiple_of(which * KVH * DH + head * DH, DH), DH)]

    for g in range(KVH):
        kv_head = meta[E_KV + g]
        vert = [kv_cols(0, kv_head), kv_cols(1, kv_head)]
        for c in range(2):
            parts = vert + [q_cols(meta[E_HEAD + g * GROUP + 2 * c + p]) for p in range(2)]
            parts += [kv_cols(c, g), q_cols(4 * g + 2 * c), q_cols(4 * g + 2 * c + 1)]
            for n, part in enumerate(parts):
                out_ref[2 * g + c, n * ROWS : (n + 1) * ROWS, :] = part


def pick_kernel(meta, vert_ref, in_ref, spread_ref, swap_ref, kv_ref):
    lo = meta[M_LO]
    g = lo >> 1
    c = lo & 1
    shard = meta[M_HI] * 2 + c
    block = jnp.int32(0)
    for p in range(GROUP):
        head = meta[M_HEAD + g * GROUP + p]
        for j in range(NV):
            v = vert_ref[head, j]
            block = jnp.where((v >> 2) == shard, v & 3, block)
    first = c * (LO // 2) + 2 * block
    for half in range(2):
        for which in range(2):
            part = in_ref[first + half, VERT + which * ROWS : VERT + (which + 1) * ROWS, :]
            at = which * BLOCK + half * ROWS
            for d in range(HI):
                spread_ref[d, at : at + ROWS, :] = part
    swap_ref[...] = in_ref[:, QDYN:QNAT, :]
    kv_ref[...] = in_ref[:, KVNAT:QNAT, :]


def scores(q, k):
    return lax.dot_general(q, k, (((1,), (1,)), ((), ())), preferred_element_type=f32)


def slash_kernel(
    meta, in_ref, swap_ref, before_ref, before_swap_ref, out_ref, stats_ref, q_ref, k_buf, v_buf
):
    half = LO * ROWS
    lo = meta[M_LO]
    core = lo & 1
    for t in range(2):
        rows = slice(t * ROWS, (t + 1) * ROWS)
        q_ref[2 * core + t] = in_ref[:, QDYN + t * ROWS : QDYN + (t + 1) * ROWS, :].reshape(half, DH)
        q_ref[2 * (1 - core) + t] = swap_ref[:, rows, :].reshape(half, DH)
    for c in range(2):

        @pl.when((lo & 1) == c)
        def _(c=c):
            mine, other = (k_buf, v_buf) if c == 0 else (v_buf, k_buf)
            mine[0:half, :] = before_ref[...].reshape(half, DH)
            other[0:half, :] = before_swap_ref[...].reshape(half, DH)
            mine[half:, :] = in_ref[:, KVNAT:QNAT, :].reshape(half, DH)
            other[half:, :] = swap_ref[:, KVNAT - QDYN :, :].reshape(half, DH)

    first_block = meta[M_HI] * 8
    band = 8 * BLOCK
    offset = 8 - lax.broadcasted_iota(jnp.int32, (1, band), 1) // BLOCK
    causal = jnp.where(
        lax.broadcasted_iota(jnp.int32, (BLOCK, BLOCK), 1)
        <= lax.broadcasted_iota(jnp.int32, (BLOCK, BLOCK), 0),
        0.0,
        -jnp.inf,
    )
    lane = lax.broadcasted_iota(jnp.int32, (BLOCK, DH), 1)
    live = []
    for a in range(2):
        mask = meta[M_MASK + 2 * lo + a]
        live.append((jnp.right_shift(jnp.full((1, band), mask, jnp.int32), offset) & 1) == 1)

    def step(i, _):
        at = pl.multiple_of(i * BLOCK, BLOCK)
        near_at = pl.multiple_of(i * BLOCK + band, BLOCK)
        reach = offset <= first_block + i
        two = pl.ds(2 * i, 2)
        q = jnp.concatenate(
            [
                in_ref[two, QNAT + a * ROWS : QNAT + (a + 1) * ROWS, :].reshape(BLOCK, DH)
                for a in range(2)
            ],
            axis=0,
        )
        far = scores(q, k_buf[pl.ds(at, band), :])
        near = scores(q, k_buf[pl.ds(near_at, BLOCK), :])
        tile = jnp.zeros((BLOCK, DH), f32)
        for a in range(2):
            rows = slice(a * BLOCK, (a + 1) * BLOCK)
            s_far = far[rows] + jnp.where(live[a] & reach, 0.0, -jnp.inf)
            s_near = near[rows] + causal
            top = jnp.maximum(
                jnp.max(s_far, axis=1, keepdims=True), jnp.max(s_near, axis=1, keepdims=True)
            )
            e_far = jnp.exp2((s_far - top) * EXP2_SCALE)
            e_near = jnp.exp2((s_near - top) * EXP2_SCALE)
            total = jnp.sum(e_far, axis=1, keepdims=True) + jnp.sum(e_near, axis=1, keepdims=True)
            acc = jnp.dot(
                e_far.astype(bf16), v_buf[pl.ds(at, band), :], preferred_element_type=f32
            ) + jnp.dot(
                e_near.astype(bf16), v_buf[pl.ds(near_at, BLOCK), :], preferred_element_type=f32
            )
            out_ref[two, a * ROWS : (a + 1) * ROWS, :] = acc.astype(bf16).reshape(2, ROWS, DH)
            tile = jnp.where(lane == GROUP + a, top, tile)
            tile = jnp.where(lane == L_LANE + GROUP + a, total, tile)
        stats_ref[two] = tile.reshape(2, ROWS, DH)
        return 0

    lax.fori_loop(0, 8, step, 0)


def vertical_kernel(
    meta,
    vert_ref,
    q_buf,
    all_ref,
    slash_ref,
    slash_stats_ref,
    out_ref,
    k_buf,
    v_buf,
    stats_buf,
):
    lo = meta[M_LO]
    g = lo >> 1
    c = lo & 1
    first_block = meta[M_HI] * 8
    tokens = LO * ROWS
    width = NV * BLOCK
    out_ref[:, OS:STATS, :] = slash_ref[...]
    stats_buf[...] = slash_stats_ref[...].reshape(tokens, DH)
    k_buf[...] = jnp.zeros(k_buf.shape, bf16)
    v_buf[...] = jnp.zeros(v_buf.shape, bf16)
    of_lane = lax.broadcasted_iota(jnp.int32, (1, width), 1) // BLOCK

    def head_step(p, _):
        head = meta[M_HEAD + g * GROUP + p]
        count = jnp.int32(0)
        ids = jnp.full((1, width), 1 << 20, jnp.int32)
        for j in range(NV):
            v = vert_ref[head, j]
            mine = ((v >> 2) & 1) == c
            source = v >> 3
            at = pl.multiple_of(count * BLOCK, BLOCK)
            k_buf[pl.ds(at, BLOCK), :] = all_ref[source, 0:BLOCK, :]
            v_buf[pl.ds(at, BLOCK), :] = all_ref[source, BLOCK : 2 * BLOCK, :]
            ids = jnp.where(of_lane == jnp.where(mine, count, NV), v, ids)
            count = count + mine.astype(jnp.int32)
        mask = jnp.full((1, width), meta[M_MASK + head], jnp.int32)

        def attend(n):
            size = n * BLOCK

            rows = LO * ROWS // STEPS
            lane = lax.broadcasted_iota(jnp.int32, (rows, DH), 1)
            for i in range(STEPS):
                span = slice(i * rows, (i + 1) * rows)
                s = scores(q_buf[p, span, :], k_buf[0:size, :])
                parts = []
                for t in range(rows // BLOCK):
                    distance = first_block + i * (rows // BLOCK) + t - ids[:, 0:size]
                    slashed = jnp.right_shift(mask[:, 0:size], jnp.clip(distance, 0, 31)) & 1
                    bias = jnp.where((distance > 0) & (slashed == 0), 0.0, -jnp.inf)
                    parts.append(s[t * BLOCK : (t + 1) * BLOCK] + bias)
                s = jnp.concatenate(parts, axis=0)
                top = jnp.maximum(jnp.max(s, axis=1, keepdims=True), LOWEST)
                e = jnp.exp2((s - top) * EXP2_SCALE)
                total = jnp.sum(e, axis=1, keepdims=True)
                acc = jnp.dot(e.astype(bf16), v_buf[0:size, :], preferred_element_type=f32)
                held = slice(i * rows // ROWS, (i + 1) * rows // ROWS)
                out_ref[held, pl.ds(pl.multiple_of(OV + p * ROWS, ROWS), ROWS), :] = acc.astype(
                    bf16
                ).reshape(rows // ROWS, ROWS, DH)
                tile = jnp.where(lane == p, top, stats_buf[span, :])
                stats_buf[span, :] = jnp.where(lane == L_LANE + p, total, tile)

        for low, n in ((-1, 8), (8, 12), (12, 16)):

            @pl.when((count > low) & (count <= n))
            def _(n=n):
                attend(n)

        return 0

    lax.fori_loop(0, GROUP, head_step, 0)
    stats = stats_buf[...]
    first = stats.astype(bf16).astype(f32)
    stats = stats - first
    second = stats.astype(bf16).astype(f32)
    third = stats - second
    packed = first + pltpu.roll(second, PART, 1) + pltpu.roll(third, 2 * PART, 1)
    out_ref[:, STATS:, :] = packed.astype(bf16).reshape(LO, ROWS, DH)


def exit_kernel(meta, in_ref, gate_ref, out_ref, m_buf, l_buf):
    row = lax.broadcasted_iota(jnp.int32, (DH, SLOTS * DH), 0)
    col = lax.broadcasted_iota(jnp.int32, (DH, SLOTS * DH), 1) // DH
    row = jnp.where(row < 3 * PART, row % PART, PART)
    m_pick = jnp.where(row == col, 1.0, 0.0).astype(bf16)
    l_pick = jnp.where(row == col + L_LANE, 1.0, 0.0).astype(bf16)
    stats = in_ref[:, STATS:, :].reshape(LO * ROWS, DH)
    m_buf[...] = jnp.dot(stats, m_pick, preferred_element_type=f32).reshape(LO, ROWS, SLOTS * DH)
    l_buf[...] = jnp.dot(stats, l_pick, preferred_element_type=f32).reshape(LO, ROWS, SLOTS * DH)

    def source_step(n, _):
        for a in range(2):
            h = 2 * n + a
            cols = slice((GROUP + a) * DH, (GROUP + a + 1) * DH)
            tops = [m_buf[n, :, cols]]
            sums = [l_buf[n, :, cols]]
            accs = [in_ref[n, OS + a * ROWS : OS + (a + 1) * ROWS, :]]
            slot = meta[M_SLOT + h]
            p = slot & 3
            lanes = pl.ds(pl.multiple_of(p * DH, DH), DH)
            for c in range(2):
                source = 2 * (slot >> 2) + c
                tops.append(m_buf[source, :, lanes])
                sums.append(l_buf[source, :, lanes])
                accs.append(in_ref[source, pl.ds(pl.multiple_of(OV + p * ROWS, ROWS), ROWS), :])
            best = jnp.maximum(jnp.maximum(tops[0], tops[1]), tops[2])
            num = jnp.zeros((ROWS, DH), f32)
            den = jnp.zeros((ROWS, DH), f32)
            for top, total, acc in zip(tops, sums, accs):
                w = jnp.exp2((top - best) * EXP2_SCALE)
                num = num + w * acc.astype(f32)
                den = den + w * total
            attended = (num / den).astype(bf16).astype(f32)
            at = pl.ds(pl.multiple_of(h * DH, DH), DH)
            gate = gate_ref[:, at].astype(f32)
            out_ref[:, at] = (jax.nn.sigmoid(gate) * attended).astype(bf16)
        return 0

    lax.fori_loop(0, LO, source_step, 0, unroll=2)


def call(kernel, out_shape, in_specs, scratch=(), **options):
    run = pl.pallas_call(
        kernel,
        out_shape=out_shape,
        in_specs=in_specs,
        out_specs=tuple(VMEM for _ in out_shape) if isinstance(out_shape, tuple) else VMEM,
        scratch_shapes=list(scratch),
        **options,
    )

    def placed(*args):
        return run(
            *(
                pltpu.with_memory_space_constraint(arg, pltpu.VMEM) if spec is VMEM else arg
                for arg, spec in zip(args, in_specs)
            )
        )

    return placed


def shape(rows, dtype=bf16, lead=LO):
    return jax.ShapeDtypeStruct((lead, rows, DH), dtype)


def in_vmem(rows, lead=LO):
    return pltpu.VMEM((lead, rows, DH), bf16)


def body(queries, key_values, gate_logits, vertical_blocks, slash_offsets, slash_count):
    entry_meta, meta = tables(vertical_blocks, slash_offsets, slash_count)
    flat_kv = key_values.reshape(ROWS, 2 * KVH * DH)
    sent = call(entry_kernel, shape(IN_ROWS), [SMEM, VMEM, VMEM])(entry_meta, queries, flat_kv)
    mine = lax.all_to_all(sent, "lo", 0, 0, tiled=True)
    spread, swap, kv_own = call(
        pick_kernel,
        (shape(2 * BLOCK, lead=HI), in_vmem(QNAT - QDYN), in_vmem(ROWS)),
        [SMEM, SMEM, VMEM],
    )(meta, vertical_blocks, mine)
    before = lax.ppermute(kv_own, ("y", "k"), [(i, i + 1) for i in range(HI - 1)])
    verticals = lax.all_to_all(spread, ("y", "k"), 0, 0, tiled=True)
    partner = [(i, i ^ 1) for i in range(LO)]
    swapped = lax.ppermute(swap, "lo", partner)
    before_swap = lax.ppermute(before, "lo", partner)
    slash, slash_stats, vertical_queries = call(
        slash_kernel,
        (shape(2 * ROWS), shape(ROWS, f32), shape(LO * ROWS, lead=GROUP)),
        [SMEM, VMEM, VMEM, VMEM, VMEM],
        [pltpu.VMEM((2 * LO * ROWS, DH), bf16)] * 2,
    )(meta, mine, swapped, before, before_swap)
    partial = call(
        vertical_kernel,
        shape(OUT_ROWS),
        [SMEM, SMEM, LOADED, VMEM, LOADED, LOADED],
        [
            pltpu.VMEM(((NV + 1) * BLOCK, DH), bf16),
            pltpu.VMEM(((NV + 1) * BLOCK, DH), bf16),
            pltpu.VMEM((LO * ROWS, DH), f32),
        ],
    )(meta, vertical_blocks, vertical_queries, verticals, slash, slash_stats)
    back = lax.all_to_all(partial, "lo", 0, 0, tiled=True)
    return call(
        exit_kernel,
        jax.ShapeDtypeStruct((ROWS, H * DH), bf16),
        [SMEM, VMEM, VMEM],
        [pltpu.VMEM((LO, ROWS, SLOTS * DH), f32)] * 2,
    )(meta, back, gate_logits)


def solution(mesh):
    pairs = Mesh(mesh.devices.reshape(NY, NK, LO), ("y", "k", "lo"))
    tokens = P(("y", "k", "lo"))

    return jax.shard_map(
        body,
        mesh=pairs,
        in_specs=(tokens, tokens, tokens, P(), P(), P()),
        out_specs=tokens,
        check_vma=False,
    )
```

```python
import jax
import jax.numpy as jnp
from jax import lax
from jax.experimental import pallas as pl
from jax.experimental.pallas import tpu as pltpu
from jax.sharding import Mesh
from jax.sharding import PartitionSpec as P

H = 32
KVH = 8
DH = 128
BLOCK = 64
NV = 16
NS = 8
ROWS = 32
LO = 16
NY = 8
NK = 4
HI = NY * NK
GROUP = 4
LOWEST = -3.0e38
STEPS = 2
EXP2_SCALE = DH**-0.5 * 1.4426950408889634

VERT, KVNAT, QDYN, QNAT, IN_ROWS = 0, 64, 0, 128, 192
KV_ROWS = QNAT - KVNAT
OV, OS, STATS, OUT_ROWS = 0, 128, 192, 208
SLOTS = GROUP + 2
L_LANE = 8
PART = 16
M_HEAD, M_SLOT, M_MASK, M_HI, M_LO, M_BLOCK = 0, 32, 64, 96, 97, 98
E_HEAD, E_KV, E_ZL = 0, 32, 40

bf16 = jnp.bfloat16
f32 = jnp.float32
SMEM = pl.BlockSpec(memory_space=pltpu.SMEM)
VMEM = pl.BlockSpec(memory_space=pltpu.VMEM)
LOADED = pl.BlockSpec(memory_space=pltpu.VMEM)


def tables(vertical_blocks, slash_offsets, slash_count):
    hi = lax.axis_index(("y", "k"))
    lo = lax.axis_index("lo")
    heads = jnp.arange(H, dtype=jnp.int32)
    groups = H // GROUP
    order = slash_count * H + heads
    rank = jnp.sum((order[None, :] < order[:, None]).astype(jnp.int32), axis=1)
    within = rank // groups
    place = rank % groups
    group = jnp.where(within % 2 == 0, place, groups - 1 - place)
    slot = group * GROUP + within
    head_of = jnp.sum(jnp.where(slot[None, :] == heads[:, None], heads[None, :], 0), axis=1)
    live = jnp.arange(NS, dtype=jnp.int32)[None, :] < slash_count[:, None]
    mask = jnp.sum(jnp.where(live, jnp.left_shift(1, slash_offsets), 0), axis=1)
    shard = hi * 2 + lo // (LO // 2)
    here = jnp.any(vertical_blocks // 4 == shard, axis=1)
    kv_of = jnp.sum(
        jnp.where(
            (group[None, :] == jnp.arange(groups, dtype=jnp.int32)[:, None]) & here[None, :],
            (heads // (H // KVH))[None, :],
            0,
        ),
        axis=1,
    )
    taken = (group == lo // 2)[:, None] & (vertical_blocks // 4 == hi * 2 + lo % 2)
    block = jnp.sum(jnp.where(taken, vertical_blocks % 4, 0))
    entry = jnp.concatenate([head_of, kv_of, (lo // (LO // 2))[None]]).astype(jnp.int32)
    rest = jnp.concatenate([head_of, slot, mask, jnp.stack([hi, lo, block])])
    return entry, rest.astype(jnp.int32)


def entry_kernel(meta, q_ref, kv_ref, out_ref):
    def q_cols(head):
        return q_ref[:, pl.ds(pl.multiple_of(head * DH, DH), DH)]

    def kv_cols(which, head):
        return kv_ref[:, pl.ds(pl.multiple_of(which * KVH * DH + head * DH, DH), DH)]

    zl = meta[E_ZL]
    for g in range(KVH):
        kv_head = meta[E_KV + g]
        near = [kv_cols(0, kv_head), kv_cols(1, kv_head), kv_cols(0, g), kv_cols(1, g)]
        far = [q_cols(meta[E_HEAD + g * GROUP + p]) for p in range(GROUP)]
        for core, parts in ((zl, near), (1 - zl, far)):
            own = [q_cols(4 * g + 2 * core + a) for a in range(2)]
            for n, part in enumerate(parts + own):
                out_ref[2 * g + core, n * ROWS : (n + 1) * ROWS, :] = part


def pick_kernel(meta, in_ref, spread_ref, swap_ref, kv_ref):
    c = meta[M_LO] & 1
    half = LO // 2
    first = c * half + 2 * meta[M_BLOCK]
    for side in range(2):
        for which in range(2):
            part = in_ref[first + side, VERT + which * ROWS : VERT + (which + 1) * ROWS, :]
            at = which * BLOCK + side * ROWS
            for d in range(HI):
                spread_ref[d, at : at + ROWS, :] = part
    kv = in_ref[pl.ds(c * half, half), KVNAT:QNAT, :]
    kv_ref[...] = kv
    swap_ref[:, 0:KV_ROWS, :] = kv
    swap_ref[:, KV_ROWS:, :] = in_ref[pl.ds((1 - c) * half, half), QDYN:QNAT, :]


def scores(q, k):
    return lax.dot_general(q, k, (((1,), (1,)), ((), ())), preferred_element_type=f32)


def slash_kernel(
    meta, in_ref, swap_ref, before_ref, before_swap_ref, out_ref, stats_ref, q_ref, k_buf, v_buf
):
    lo = meta[M_LO]
    core = lo & 1
    some = LO // 2
    shard = some * ROWS
    pair = 2 * shard
    mine = pl.multiple_of(core * shard, shard)
    other = pl.multiple_of((1 - core) * shard, shard)
    far = pl.ds((1 - core) * some, some)
    near = pl.ds(core * some, some)
    for p in range(GROUP):
        rows = slice(p * ROWS, (p + 1) * ROWS)
        q_ref[p, pl.ds(other, shard), :] = in_ref[far, rows, :].reshape(shard, DH)
        rows = slice(KV_ROWS + p * ROWS, KV_ROWS + (p + 1) * ROWS)
        q_ref[p, pl.ds(mine, shard), :] = swap_ref[:, rows, :].reshape(shard, DH)
    for n, buf in enumerate((k_buf, v_buf)):
        rows = slice(n * ROWS, (n + 1) * ROWS)
        buf[pl.ds(mine, shard), :] = before_ref[:, rows, :].reshape(shard, DH)
        buf[pl.ds(other, shard), :] = before_swap_ref[:, rows, :].reshape(shard, DH)
        held = slice(KVNAT + n * ROWS, KVNAT + (n + 1) * ROWS)
        buf[pl.ds(pair + mine, shard), :] = in_ref[near, held, :].reshape(shard, DH)
        buf[pl.ds(pair + other, shard), :] = swap_ref[:, rows, :].reshape(shard, DH)

    first_block = meta[M_HI] * 8
    band = 8 * BLOCK
    offset = 8 - lax.broadcasted_iota(jnp.int32, (1, band), 1) // BLOCK
    causal = jnp.where(
        lax.broadcasted_iota(jnp.int32, (BLOCK, BLOCK), 1)
        <= lax.broadcasted_iota(jnp.int32, (BLOCK, BLOCK), 0),
        0.0,
        -jnp.inf,
    )
    lane = lax.broadcasted_iota(jnp.int32, (BLOCK, DH), 1)
    live = []
    for a in range(2):
        mask = meta[M_MASK + 2 * lo + a]
        live.append((jnp.right_shift(jnp.full((1, band), mask, jnp.int32), offset) & 1) == 1)

    def step(i, _):
        at = pl.multiple_of(i * BLOCK, BLOCK)
        near_at = pl.multiple_of(i * BLOCK + band, BLOCK)
        reach = offset <= first_block + i
        two = pl.ds(2 * i, 2)
        q = jnp.concatenate(
            [
                in_ref[two, QNAT + a * ROWS : QNAT + (a + 1) * ROWS, :].reshape(BLOCK, DH)
                for a in range(2)
            ],
            axis=0,
        )
        far = scores(q, k_buf[pl.ds(at, band), :])
        near = scores(q, k_buf[pl.ds(near_at, BLOCK), :])
        tile = jnp.zeros((BLOCK, DH), f32)
        for a in range(2):
            rows = slice(a * BLOCK, (a + 1) * BLOCK)
            s_far = far[rows] + jnp.where(live[a] & reach, 0.0, -jnp.inf)
            s_near = near[rows] + causal
            top = jnp.maximum(
                jnp.max(s_far, axis=1, keepdims=True), jnp.max(s_near, axis=1, keepdims=True)
            )
            e_far = jnp.exp2((s_far - top) * EXP2_SCALE)
            e_near = jnp.exp2((s_near - top) * EXP2_SCALE)
            total = jnp.sum(e_far, axis=1, keepdims=True) + jnp.sum(e_near, axis=1, keepdims=True)
            acc = jnp.dot(
                e_far.astype(bf16), v_buf[pl.ds(at, band), :], preferred_element_type=f32
            ) + jnp.dot(
                e_near.astype(bf16), v_buf[pl.ds(near_at, BLOCK), :], preferred_element_type=f32
            )
            out_ref[two, a * ROWS : (a + 1) * ROWS, :] = acc.astype(bf16).reshape(2, ROWS, DH)
            tile = jnp.where(lane == GROUP + a, top, tile)
            tile = jnp.where(lane == L_LANE + GROUP + a, total, tile)
        stats_ref[two] = tile.reshape(2, ROWS, DH)
        return 0

    lax.fori_loop(0, 8, step, 0)


def vertical_kernel(
    meta,
    vert_ref,
    q_buf,
    all_ref,
    slash_ref,
    slash_stats_ref,
    out_ref,
    k_buf,
    v_buf,
    stats_buf,
    bias_buf,
):
    lo = meta[M_LO]
    g = lo >> 1
    c = lo & 1
    first_block = meta[M_HI] * 8
    tokens = LO * ROWS
    width = NV * BLOCK
    out_ref[:, OS:STATS, :] = slash_ref[...]
    stats_buf[...] = slash_stats_ref[...].reshape(tokens, DH)
    k_buf[...] = jnp.zeros(k_buf.shape, bf16)
    v_buf[...] = jnp.zeros(v_buf.shape, bf16)
    of_lane = lax.broadcasted_iota(jnp.int32, (1, width), 1) // BLOCK

    def head_step(p, _):
        head = meta[M_HEAD + g * GROUP + p]
        count = jnp.int32(0)
        ids = jnp.full((1, width), 1 << 20, jnp.int32)
        for j in range(NV):
            v = vert_ref[head, j]
            mine = ((v >> 2) & 1) == c
            source = v >> 3
            at = pl.multiple_of(count * BLOCK, BLOCK)
            k_buf[pl.ds(at, BLOCK), :] = all_ref[source, 0:BLOCK, :]
            v_buf[pl.ds(at, BLOCK), :] = all_ref[source, BLOCK : 2 * BLOCK, :]
            ids = jnp.where(of_lane == jnp.where(mine, count, NV), v, ids)
            count = count + mine.astype(jnp.int32)
        block_of_row = lax.broadcasted_iota(jnp.int32, (8, width), 0) + first_block
        distance = block_of_row - ids
        mask = jnp.full((8, width), meta[M_MASK + head], jnp.int32)
        slashed = jnp.right_shift(mask, jnp.clip(distance, 0, 31)) & 1
        bias_buf[...] = jnp.where((distance > 0) & (slashed == 0), 0.0, -jnp.inf)

        def attend(n):
            size = n * BLOCK

            rows = LO * ROWS // STEPS
            lane = lax.broadcasted_iota(jnp.int32, (rows, DH), 1)
            for i in range(STEPS):
                span = slice(i * rows, (i + 1) * rows)
                s = scores(q_buf[p, span, :], k_buf[0:size, :])
                parts = []
                for t in range(rows // BLOCK):
                    at = i * (rows // BLOCK) + t
                    bias = bias_buf[at : at + 1, 0:size]
                    parts.append(s[t * BLOCK : (t + 1) * BLOCK] + bias)
                s = jnp.concatenate(parts, axis=0)
                top = jnp.maximum(jnp.max(s, axis=1, keepdims=True), LOWEST)
                e = jnp.exp2((s - top) * EXP2_SCALE)
                total = jnp.sum(e, axis=1, keepdims=True)
                acc = jnp.dot(e.astype(bf16), v_buf[0:size, :], preferred_element_type=f32)
                held = slice(i * rows // ROWS, (i + 1) * rows // ROWS)
                out_ref[held, pl.ds(pl.multiple_of(OV + p * ROWS, ROWS), ROWS), :] = acc.astype(
                    bf16
                ).reshape(rows // ROWS, ROWS, DH)
                tile = jnp.where(lane == p, top, stats_buf[span, :])
                stats_buf[span, :] = jnp.where(lane == L_LANE + p, total, tile)

        for low, n in ((-1, 8), (8, 12), (12, 16)):

            @pl.when((count > low) & (count <= n))
            def _(n=n):
                attend(n)

        return 0

    lax.fori_loop(0, GROUP, head_step, 0)
    stats = stats_buf[...]
    first = stats.astype(bf16).astype(f32)
    stats = stats - first
    second = stats.astype(bf16).astype(f32)
    third = stats - second
    packed = first + pltpu.roll(second, PART, 1) + pltpu.roll(third, 2 * PART, 1)
    packed = packed.reshape(LO, ROWS, DH)
    low = packed[:, 0 : ROWS // 2, :].reshape(LO * ROWS // 2, DH)
    high = packed[:, ROWS // 2 :, :].reshape(LO * ROWS // 2, DH)
    packed = low + pltpu.roll(high, DH // 2, 1)
    out_ref[:, STATS:, :] = packed.astype(bf16).reshape(LO, ROWS // 2, DH)


def exit_kernel(meta, in_ref, gate_ref, out_ref, m_buf, l_buf):
    row = lax.broadcasted_iota(jnp.int32, (DH, SLOTS * DH), 0)
    col = lax.broadcasted_iota(jnp.int32, (DH, SLOTS * DH), 1) // DH
    stats = in_ref[:, STATS:, :].reshape(LO * ROWS // 2, DH)
    for side in range(2):
        at = row - side * (DH // 2)
        value = jnp.where((at >= 0) & (at < 3 * PART), at & (PART - 1), PART)
        held = slice(side * ROWS // 2, (side + 1) * ROWS // 2)
        for buf, lane in ((m_buf, 0), (l_buf, L_LANE)):
            pick = jnp.where(value == col + lane, 1.0, 0.0).astype(bf16)
            buf[:, held, :] = jnp.dot(stats, pick, preferred_element_type=f32).reshape(
                LO, ROWS // 2, SLOTS * DH
            )

    def source_step(n, _):
        for a in range(2):
            h = 2 * n + a
            cols = slice((GROUP + a) * DH, (GROUP + a + 1) * DH)
            tops = [m_buf[n, :, cols]]
            sums = [l_buf[n, :, cols]]
            accs = [in_ref[n, OS + a * ROWS : OS + (a + 1) * ROWS, :]]
            slot = meta[M_SLOT + h]
            p = slot & 3
            lanes = pl.ds(pl.multiple_of(p * DH, DH), DH)
            for c in range(2):
                source = 2 * (slot >> 2) + c
                tops.append(m_buf[source, :, lanes])
                sums.append(l_buf[source, :, lanes])
                accs.append(in_ref[source, pl.ds(pl.multiple_of(OV + p * ROWS, ROWS), ROWS), :])
            best = jnp.maximum(jnp.maximum(tops[0], tops[1]), tops[2])
            num = jnp.zeros((ROWS, DH), f32)
            den = jnp.zeros((ROWS, DH), f32)
            for top, total, acc in zip(tops, sums, accs):
                w = jnp.exp2((top - best) * EXP2_SCALE)
                num = num + w * acc.astype(f32)
                den = den + w * total
            attended = (num / den).astype(bf16).astype(f32)
            at = pl.ds(pl.multiple_of(h * DH, DH), DH)
            gate = gate_ref[:, at].astype(f32)
            out_ref[:, at] = (jax.nn.sigmoid(gate) * attended).astype(bf16)
        return 0

    lax.fori_loop(0, LO, source_step, 0, unroll=2)


def call(kernel, out_shape, in_specs, scratch=(), **options):
    run = pl.pallas_call(
        kernel,
        out_shape=out_shape,
        in_specs=in_specs,
        out_specs=tuple(VMEM for _ in out_shape) if isinstance(out_shape, tuple) else VMEM,
        scratch_shapes=list(scratch),
        **options,
    )

    def placed(*args):
        return run(
            *(
                pltpu.with_memory_space_constraint(arg, pltpu.VMEM) if spec is VMEM else arg
                for arg, spec in zip(args, in_specs)
            )
        )

    return placed


def shape(rows, dtype=bf16, lead=LO):
    return jax.ShapeDtypeStruct((lead, rows, DH), dtype)


def in_vmem(rows, lead=LO):
    return pltpu.VMEM((lead, rows, DH), bf16)


def body(queries, key_values, gate_logits, vertical_blocks, slash_offsets, slash_count):
    entry_meta, meta = tables(vertical_blocks, slash_offsets, slash_count)
    flat_kv = key_values.reshape(ROWS, 2 * KVH * DH)
    sent = call(entry_kernel, shape(IN_ROWS), [SMEM, VMEM, VMEM])(entry_meta, queries, flat_kv)
    mine = lax.all_to_all(sent, "lo", 0, 0, tiled=True)
    spread, swap, kv_own = call(
        pick_kernel,
        (
            shape(2 * BLOCK, lead=HI),
            in_vmem(KV_ROWS + QNAT, lead=LO // 2),
            in_vmem(KV_ROWS, lead=LO // 2),
        ),
        [SMEM, VMEM],
    )(meta, mine)
    before = lax.ppermute(kv_own, ("y", "k"), [(i, i + 1) for i in range(HI - 1)])
    verticals = lax.all_to_all(spread, ("y", "k"), 0, 0, tiled=True)
    partner = [(i, i ^ 1) for i in range(LO)]
    swapped = lax.ppermute(swap, "lo", partner)
    before_swap = lax.ppermute(before, "lo", partner)
    slash, slash_stats, vertical_queries = call(
        slash_kernel,
        (shape(2 * ROWS), shape(ROWS, f32), shape(LO * ROWS, lead=GROUP)),
        [SMEM, VMEM, VMEM, VMEM, VMEM],
        [pltpu.VMEM((2 * LO * ROWS, DH), bf16)] * 2,
    )(meta, mine, swapped, before, before_swap)
    partial = call(
        vertical_kernel,
        in_vmem(OUT_ROWS),
        [SMEM, SMEM, LOADED, VMEM, LOADED, LOADED],
        [
            pltpu.VMEM(((NV + 1) * BLOCK, DH), bf16),
            pltpu.VMEM(((NV + 1) * BLOCK, DH), bf16),
            pltpu.VMEM((LO * ROWS, DH), f32),
            pltpu.VMEM((8, NV * BLOCK), f32),
        ],
    )(meta, vertical_blocks, vertical_queries, verticals, slash, slash_stats)
    back = lax.all_to_all(partial, "lo", 0, 0, tiled=True)
    return call(
        exit_kernel,
        jax.ShapeDtypeStruct((ROWS, H * DH), bf16),
        [SMEM, VMEM, VMEM],
        [pltpu.VMEM((LO, ROWS, SLOTS * DH), f32)] * 2,
    )(meta, back, gate_logits)


def solution(mesh):
    pairs = Mesh(mesh.devices.reshape(NY, NK, LO), ("y", "k", "lo"))
    tokens = P(("y", "k", "lo"))

    return jax.shard_map(
        body,
        mesh=pairs,
        in_specs=(tokens, tokens, tokens, P(), P(), P()),
        out_specs=tokens,
        check_vma=False,
    )
```

```python
import jax
import jax.numpy as jnp
from jax import lax
from jax.experimental import pallas as pl
from jax.experimental.pallas import tpu as pltpu
from jax.sharding import Mesh
from jax.sharding import PartitionSpec as P

H = 32
KVH = 8
DH = 128
BLOCK = 64
NV = 16
NS = 8
ROWS = 32
LO = 16
NY = 8
NK = 4
HI = NY * NK
GROUP = 4
LOWEST = -3.0e38
STEPS = 2
EXP2_SCALE = DH**-0.5 * 1.4426950408889634

VERT, KVNAT, QDYN, QNAT, IN_ROWS = 0, 64, 0, 128, 192
KV_ROWS = QNAT - KVNAT
OV, OS, STATS, OUT_ROWS = 0, 128, 192, 208
SLOTS = GROUP + 2
L_LANE = 8
PART = 16
M_HEAD, M_SLOT, M_MASK, M_HI, M_LO, M_BLOCK = 0, 32, 64, 96, 97, 98

bf16 = jnp.bfloat16
f32 = jnp.float32
SMEM = pl.BlockSpec(memory_space=pltpu.SMEM)
VMEM = pl.BlockSpec(memory_space=pltpu.VMEM)
LOADED = pl.BlockSpec(memory_space=pltpu.VMEM)


def tables(vertical_blocks, slash_offsets, slash_count):
    hi = lax.axis_index(("y", "k"))
    lo = lax.axis_index("lo")
    heads = jnp.arange(H, dtype=jnp.int32)
    groups = H // GROUP
    order = slash_count * H + heads
    rank = jnp.sum((order[None, :] < order[:, None]).astype(jnp.int32), axis=1)
    within = rank // groups
    place = rank % groups
    group = jnp.where(within % 2 == 0, place, groups - 1 - place)
    slot = group * GROUP + within
    head_of = jnp.sum(jnp.where(slot[None, :] == heads[:, None], heads[None, :], 0), axis=1)
    live = jnp.arange(NS, dtype=jnp.int32)[None, :] < slash_count[:, None]
    mask = jnp.sum(jnp.where(live, jnp.left_shift(1, slash_offsets), 0), axis=1)
    taken = (group == lo // 2)[:, None] & (vertical_blocks // 4 == hi * 2 + lo % 2)
    block = jnp.sum(jnp.where(taken, vertical_blocks % 4, 0))
    rest = jnp.concatenate([head_of, slot, mask, jnp.stack([hi, lo, block])])
    return rest.astype(jnp.int32)


def entry_tables(count_ref, vert_ref, shard, start, head_of, kv_of):
    head = lax.broadcasted_iota(jnp.int32, vert_ref.shape, 1)
    weight = jnp.left_shift(1, head & 15).astype(f32)
    hit = jnp.where((vert_ref[...] >> 2) == shard, weight, 0.0)
    here = [
        jnp.sum(jnp.where((head >> 4) == part, hit, 0.0)).astype(jnp.int32) for part in range(2)
    ]
    for n in range(NS + 1):
        start[n] = 0
    for h in range(H):
        start[count_ref[h]] = start[count_ref[h]] + 1
    before = jnp.int32(0)
    for n in range(NS + 1):
        held = start[n]
        start[n] = before
        before = before + held
    groups = H // GROUP
    for h in range(H):
        rank = start[count_ref[h]]
        start[count_ref[h]] = rank + 1
        within = rank >> 3
        place = rank & (groups - 1)
        group = jnp.where((within & 1) == 0, place, groups - 1 - place)
        head_of[group * GROUP + within] = h
        kv_of[jnp.where(((here[h >> 4] >> (h & 15)) & 1) == 1, group, groups)] = h // (H // KVH)


def entry_kernel(count_ref, vert_ref, q_ref, kv_ref, out_ref, start, head_of, kv_of):
    lo = lax.axis_index("lo")
    zl = lo >> 3
    shard = (lax.axis_index("y") * NK + lax.axis_index("k")) * 2 + zl
    for g in range(KVH):
        kv_of[g] = 0
    entry_tables(count_ref, vert_ref, shard, start, head_of, kv_of)

    def q_cols(head):
        return q_ref[:, pl.ds(pl.multiple_of(head * DH, DH), DH)]

    def kv_cols(which, head):
        return kv_ref[:, pl.ds(pl.multiple_of(which * KVH * DH + head * DH, DH), DH)]

    for g in range(KVH):
        kv_head = kv_of[g]
        near = [kv_cols(0, kv_head), kv_cols(1, kv_head), kv_cols(0, g), kv_cols(1, g)]
        far = [q_cols(head_of[g * GROUP + p]) for p in range(GROUP)]
        for core, parts in ((zl, near), (1 - zl, far)):
            own = [q_cols(4 * g + 2 * core + a) for a in range(2)]
            for n, part in enumerate(parts + own):
                out_ref[2 * g + core, n * ROWS : (n + 1) * ROWS, :] = part


def pick_kernel(meta, in_ref, spread_ref, swap_ref, kv_ref):
    c = meta[M_LO] & 1
    half = LO // 2
    first = c * half + 2 * meta[M_BLOCK]
    for side in range(2):
        for which in range(2):
            part = in_ref[first + side, VERT + which * ROWS : VERT + (which + 1) * ROWS, :]
            at = which * BLOCK + side * ROWS
            for d in range(HI):
                spread_ref[d, at : at + ROWS, :] = part
    kv = in_ref[pl.ds(c * half, half), KVNAT:QNAT, :]
    kv_ref[...] = kv
    swap_ref[:, 0:KV_ROWS, :] = kv
    swap_ref[:, KV_ROWS:, :] = in_ref[pl.ds((1 - c) * half, half), QDYN:QNAT, :]


def scores(q, k):
    return lax.dot_general(q, k, (((1,), (1,)), ((), ())), preferred_element_type=f32)


def slash_kernel(
    meta, in_ref, swap_ref, before_ref, before_swap_ref, out_ref, stats_ref, q_ref, k_buf, v_buf
):
    lo = meta[M_LO]
    core = lo & 1
    some = LO // 2
    shard = some * ROWS
    pair = 2 * shard
    mine = pl.multiple_of(core * shard, shard)
    other = pl.multiple_of((1 - core) * shard, shard)
    far = pl.ds((1 - core) * some, some)
    near = pl.ds(core * some, some)
    for p in range(GROUP):
        rows = slice(p * ROWS, (p + 1) * ROWS)
        q_ref[p, pl.ds(other, shard), :] = in_ref[far, rows, :].reshape(shard, DH)
        rows = slice(KV_ROWS + p * ROWS, KV_ROWS + (p + 1) * ROWS)
        q_ref[p, pl.ds(mine, shard), :] = swap_ref[:, rows, :].reshape(shard, DH)
    for n, buf in enumerate((k_buf, v_buf)):
        rows = slice(n * ROWS, (n + 1) * ROWS)
        buf[pl.ds(mine, shard), :] = before_ref[:, rows, :].reshape(shard, DH)
        buf[pl.ds(other, shard), :] = before_swap_ref[:, rows, :].reshape(shard, DH)
        held = slice(KVNAT + n * ROWS, KVNAT + (n + 1) * ROWS)
        buf[pl.ds(pair + mine, shard), :] = in_ref[near, held, :].reshape(shard, DH)
        buf[pl.ds(pair + other, shard), :] = swap_ref[:, rows, :].reshape(shard, DH)

    first_block = meta[M_HI] * 8
    band = 8 * BLOCK
    offset = 8 - lax.broadcasted_iota(jnp.int32, (1, band), 1) // BLOCK
    causal = jnp.where(
        lax.broadcasted_iota(jnp.int32, (BLOCK, BLOCK), 1)
        <= lax.broadcasted_iota(jnp.int32, (BLOCK, BLOCK), 0),
        0.0,
        -jnp.inf,
    )
    lane = lax.broadcasted_iota(jnp.int32, (BLOCK, DH), 1)
    live = []
    for a in range(2):
        mask = meta[M_MASK + 2 * lo + a]
        live.append((jnp.right_shift(jnp.full((1, band), mask, jnp.int32), offset) & 1) == 1)

    def step(i, _):
        at = pl.multiple_of(i * BLOCK, BLOCK)
        near_at = pl.multiple_of(i * BLOCK + band, BLOCK)
        reach = offset <= first_block + i
        two = pl.ds(2 * i, 2)
        q = jnp.concatenate(
            [
                in_ref[two, QNAT + a * ROWS : QNAT + (a + 1) * ROWS, :].reshape(BLOCK, DH)
                for a in range(2)
            ],
            axis=0,
        )
        far = scores(q, k_buf[pl.ds(at, band), :])
        near = scores(q, k_buf[pl.ds(near_at, BLOCK), :])
        tile = jnp.zeros((BLOCK, DH), f32)
        for a in range(2):
            rows = slice(a * BLOCK, (a + 1) * BLOCK)
            s_far = far[rows] + jnp.where(live[a] & reach, 0.0, -jnp.inf)
            s_near = near[rows] + causal
            top = jnp.maximum(
                jnp.max(s_far, axis=1, keepdims=True), jnp.max(s_near, axis=1, keepdims=True)
            )
            e_far = jnp.exp2((s_far - top) * EXP2_SCALE)
            e_near = jnp.exp2((s_near - top) * EXP2_SCALE)
            total = jnp.sum(e_far, axis=1, keepdims=True) + jnp.sum(e_near, axis=1, keepdims=True)
            acc = jnp.dot(
                e_far.astype(bf16), v_buf[pl.ds(at, band), :], preferred_element_type=f32
            ) + jnp.dot(
                e_near.astype(bf16), v_buf[pl.ds(near_at, BLOCK), :], preferred_element_type=f32
            )
            out_ref[two, a * ROWS : (a + 1) * ROWS, :] = acc.astype(bf16).reshape(2, ROWS, DH)
            tile = jnp.where(lane == GROUP + a, top, tile)
            tile = jnp.where(lane == L_LANE + GROUP + a, total, tile)
        stats_ref[two] = tile.reshape(2, ROWS, DH)
        return 0

    lax.fori_loop(0, 8, step, 0)


def vertical_kernel(
    meta,
    vert_ref,
    q_buf,
    all_ref,
    slash_ref,
    slash_stats_ref,
    out_ref,
    k_buf,
    v_buf,
    stats_buf,
    bias_buf,
):
    lo = meta[M_LO]
    g = lo >> 1
    c = lo & 1
    first_block = meta[M_HI] * 8
    tokens = LO * ROWS
    width = NV * BLOCK
    out_ref[:, OS:STATS, :] = slash_ref[...]
    stats_buf[...] = slash_stats_ref[...].reshape(tokens, DH)
    k_buf[...] = jnp.zeros(k_buf.shape, bf16)
    v_buf[...] = jnp.zeros(v_buf.shape, bf16)
    of_lane = lax.broadcasted_iota(jnp.int32, (1, width), 1) // BLOCK

    def head_step(p, _):
        head = meta[M_HEAD + g * GROUP + p]
        count = jnp.int32(0)
        ids = jnp.full((1, width), 1 << 20, jnp.int32)
        for j in range(NV):
            v = vert_ref[j, head]
            mine = ((v >> 2) & 1) == c
            source = v >> 3
            at = pl.multiple_of(count * BLOCK, BLOCK)
            k_buf[pl.ds(at, BLOCK), :] = all_ref[source, 0:BLOCK, :]
            v_buf[pl.ds(at, BLOCK), :] = all_ref[source, BLOCK : 2 * BLOCK, :]
            ids = jnp.where(of_lane == jnp.where(mine, count, NV), v, ids)
            count = count + mine.astype(jnp.int32)
        block_of_row = lax.broadcasted_iota(jnp.int32, (8, width), 0) + first_block
        distance = block_of_row - ids
        mask = jnp.full((8, width), meta[M_MASK + head], jnp.int32)
        slashed = jnp.right_shift(mask, jnp.clip(distance, 0, 31)) & 1
        bias_buf[...] = jnp.where((distance > 0) & (slashed == 0), 0.0, -jnp.inf)

        def attend(n):
            size = n * BLOCK

            rows = LO * ROWS // STEPS
            lane = lax.broadcasted_iota(jnp.int32, (rows, DH), 1)
            for i in range(STEPS):
                span = slice(i * rows, (i + 1) * rows)
                s = scores(q_buf[p, span, :], k_buf[0:size, :])
                parts = []
                for t in range(rows // BLOCK):
                    at = i * (rows // BLOCK) + t
                    bias = bias_buf[at : at + 1, 0:size]
                    parts.append(s[t * BLOCK : (t + 1) * BLOCK] + bias)
                s = jnp.concatenate(parts, axis=0)
                top = jnp.maximum(jnp.max(s, axis=1, keepdims=True), LOWEST)
                e = jnp.exp2((s - top) * EXP2_SCALE)
                total = jnp.sum(e, axis=1, keepdims=True)
                acc = jnp.dot(e.astype(bf16), v_buf[0:size, :], preferred_element_type=f32)
                held = slice(i * rows // ROWS, (i + 1) * rows // ROWS)
                out_ref[held, pl.ds(pl.multiple_of(OV + p * ROWS, ROWS), ROWS), :] = acc.astype(
                    bf16
                ).reshape(rows // ROWS, ROWS, DH)
                tile = jnp.where(lane == p, top, stats_buf[span, :])
                stats_buf[span, :] = jnp.where(lane == L_LANE + p, total, tile)

        for low, n in ((-1, 8), (8, 12), (12, 16)):

            @pl.when((count > low) & (count <= n))
            def _(n=n):
                attend(n)

        return 0

    lax.fori_loop(0, GROUP, head_step, 0)
    stats = stats_buf[...]
    first = stats.astype(bf16).astype(f32)
    stats = stats - first
    second = stats.astype(bf16).astype(f32)
    third = stats - second
    packed = first + pltpu.roll(second, PART, 1) + pltpu.roll(third, 2 * PART, 1)
    packed = packed.reshape(LO, ROWS, DH)
    low = packed[:, 0 : ROWS // 2, :].reshape(LO * ROWS // 2, DH)
    high = packed[:, ROWS // 2 :, :].reshape(LO * ROWS // 2, DH)
    packed = low + pltpu.roll(high, DH // 2, 1)
    out_ref[:, STATS:, :] = packed.astype(bf16).reshape(LO, ROWS // 2, DH)


def exit_kernel(meta, in_ref, gate_ref, out_ref, m_buf, l_buf):
    row = lax.broadcasted_iota(jnp.int32, (DH, SLOTS * DH), 0)
    col = lax.broadcasted_iota(jnp.int32, (DH, SLOTS * DH), 1) // DH
    stats = in_ref[:, STATS:, :].reshape(LO * ROWS // 2, DH)
    for side in range(2):
        at = row - side * (DH // 2)
        value = jnp.where((at >= 0) & (at < 3 * PART), at & (PART - 1), PART)
        held = slice(side * ROWS // 2, (side + 1) * ROWS // 2)
        for buf, lane in ((m_buf, 0), (l_buf, L_LANE)):
            pick = jnp.where(value == col + lane, 1.0, 0.0).astype(bf16)
            buf[:, held, :] = jnp.dot(stats, pick, preferred_element_type=f32).reshape(
                LO, ROWS // 2, SLOTS * DH
            )

    for n in range(LO):
        for a in range(2):
            h = 2 * n + a
            cols = slice((GROUP + a) * DH, (GROUP + a + 1) * DH)
            tops = [m_buf[n, :, cols]]
            sums = [l_buf[n, :, cols]]
            accs = [in_ref[n, OS + a * ROWS : OS + (a + 1) * ROWS, :]]
            slot = meta[M_SLOT + h]
            p = slot & 3
            lanes = pl.ds(pl.multiple_of(p * DH, DH), DH)
            for c in range(2):
                source = 2 * (slot >> 2) + c
                tops.append(m_buf[source, :, lanes])
                sums.append(l_buf[source, :, lanes])
                accs.append(in_ref[source, pl.ds(pl.multiple_of(OV + p * ROWS, ROWS), ROWS), :])
            best = jnp.maximum(jnp.maximum(tops[0], tops[1]), tops[2])
            num = jnp.zeros((ROWS, DH), f32)
            den = jnp.zeros((ROWS, DH), f32)
            for top, total, acc in zip(tops, sums, accs):
                w = jnp.exp2((top - best) * EXP2_SCALE)
                num = num + w * acc.astype(f32)
                den = den + w * total
            attended = (num / den).astype(bf16).astype(f32)
            at = slice(h * DH, (h + 1) * DH)
            gate = gate_ref[:, at].astype(f32)
            out_ref[:, at] = (jax.nn.sigmoid(gate) * attended).astype(bf16)


def call(kernel, out_shape, in_specs, scratch=(), **options):
    run = pl.pallas_call(
        kernel,
        out_shape=out_shape,
        in_specs=in_specs,
        out_specs=tuple(VMEM for _ in out_shape) if isinstance(out_shape, tuple) else VMEM,
        scratch_shapes=list(scratch),
        **options,
    )

    def placed(*args):
        return run(
            *(
                pltpu.with_memory_space_constraint(arg, pltpu.VMEM) if spec is VMEM else arg
                for arg, spec in zip(args, in_specs)
            )
        )

    return placed


def shape(rows, dtype=bf16, lead=LO):
    return jax.ShapeDtypeStruct((lead, rows, DH), dtype)


def in_vmem(rows, lead=LO):
    return pltpu.VMEM((lead, rows, DH), bf16)


def body(queries, key_values, gate_logits, vertical_blocks, slash_offsets, slash_count):
    meta = tables(vertical_blocks, slash_offsets, slash_count)
    vertical_ids = vertical_blocks.T
    flat_kv = key_values.reshape(ROWS, 2 * KVH * DH)
    sent = call(
        entry_kernel,
        shape(IN_ROWS),
        [SMEM, LOADED, VMEM, VMEM],
        [pltpu.SMEM((16,), jnp.int32), pltpu.SMEM((H,), jnp.int32), pltpu.SMEM((16,), jnp.int32)],
    )(slash_count, vertical_ids, queries, flat_kv)
    mine = lax.all_to_all(sent, "lo", 0, 0, tiled=True)
    spread, swap, kv_own = call(
        pick_kernel,
        (
            shape(2 * BLOCK, lead=HI),
            in_vmem(KV_ROWS + QNAT, lead=LO // 2),
            in_vmem(KV_ROWS, lead=LO // 2),
        ),
        [SMEM, VMEM],
    )(meta, mine)
    before = lax.ppermute(kv_own, ("y", "k"), [(i, i + 1) for i in range(HI - 1)])
    verticals = lax.all_to_all(spread, ("y", "k"), 0, 0, tiled=True)
    partner = [(i, i ^ 1) for i in range(LO)]
    swapped = lax.ppermute(swap, "lo", partner)
    before_swap = lax.ppermute(before, "lo", partner)
    slash, slash_stats, vertical_queries = call(
        slash_kernel,
        (shape(2 * ROWS), shape(ROWS, f32), shape(LO * ROWS, lead=GROUP)),
        [SMEM, VMEM, VMEM, VMEM, VMEM],
        [pltpu.VMEM((2 * LO * ROWS, DH), bf16)] * 2,
    )(meta, mine, swapped, before, before_swap)
    partial = call(
        vertical_kernel,
        in_vmem(OUT_ROWS),
        [SMEM, SMEM, LOADED, VMEM, LOADED, LOADED],
        [
            pltpu.VMEM(((NV + 1) * BLOCK, DH), bf16),
            pltpu.VMEM(((NV + 1) * BLOCK, DH), bf16),
            pltpu.VMEM((LO * ROWS, DH), f32),
            pltpu.VMEM((8, NV * BLOCK), f32),
        ],
    )(meta, vertical_ids, vertical_queries, verticals, slash, slash_stats)
    back = lax.all_to_all(partial, "lo", 0, 0, tiled=True)
    return call(
        exit_kernel,
        jax.ShapeDtypeStruct((ROWS, H * DH), bf16),
        [SMEM, VMEM, VMEM],
        [pltpu.VMEM((LO, ROWS, SLOTS * DH), f32)] * 2,
    )(meta, back, gate_logits)


def solution(mesh):
    pairs = Mesh(mesh.devices.reshape(NY, NK, LO), ("y", "k", "lo"))
    tokens = P(("y", "k", "lo"))

    return jax.shard_map(
        body,
        mesh=pairs,
        in_specs=(tokens, tokens, tokens, P(), P(), P()),
        out_specs=tokens,
        check_vma=False,
    )
```

```python
import jax
import jax.numpy as jnp
from jax import lax
from jax.experimental import pallas as pl
from jax.experimental.pallas import tpu as pltpu
from jax.sharding import Mesh
from jax.sharding import PartitionSpec as P

H = 32
KVH = 8
DH = 128
BLOCK = 64
NV = 16
NS = 8
ROWS = 32
LO = 16
NY = 8
NK = 4
HI = NY * NK
GROUP = 4
LOWEST = -3.0e38
STEPS = 4
EXP2_SCALE = DH**-0.5 * 1.4426950408889634

VERT, KVNAT, QDYN, QNAT, IN_ROWS = 0, 64, 0, 128, 192
KV_ROWS = QNAT - KVNAT
OV, OS, STATS, OUT_ROWS = 0, 128, 192, 208
SLOTS = GROUP + 2
L_LANE = 8
PART = 16
M_HEAD, M_SLOT, M_MASK, M_HI, M_LO, M_BLOCK = 0, 32, 64, 96, 97, 98

bf16 = jnp.bfloat16
f32 = jnp.float32
SMEM = pl.BlockSpec(memory_space=pltpu.SMEM)
VMEM = pl.BlockSpec(memory_space=pltpu.VMEM)
LOADED = pl.BlockSpec(memory_space=pltpu.VMEM)


def tables(vertical_blocks, slash_offsets, slash_count):
    hi = lax.axis_index(("y", "k"))
    lo = lax.axis_index("lo")
    heads = jnp.arange(H, dtype=jnp.int32)
    groups = H // GROUP
    order = slash_count * H + heads
    rank = jnp.sum((order[None, :] < order[:, None]).astype(jnp.int32), axis=1)
    within = rank // groups
    place = rank % groups
    group = jnp.where(within % 2 == 0, place, groups - 1 - place)
    slot = group * GROUP + within
    head_of = jnp.sum(jnp.where(slot[None, :] == heads[:, None], heads[None, :], 0), axis=1)
    live = jnp.arange(NS, dtype=jnp.int32)[None, :] < slash_count[:, None]
    mask = jnp.sum(jnp.where(live, jnp.left_shift(1, slash_offsets), 0), axis=1)
    taken = (group == lo // 2)[:, None] & (vertical_blocks // 4 == hi * 2 + lo % 2)
    block = jnp.sum(jnp.where(taken, vertical_blocks % 4, 0))
    rest = jnp.concatenate([head_of, slot, mask, jnp.stack([hi, lo, block])])
    return rest.astype(jnp.int32)


def entry_tables(count_ref, vert_ref, shard, start, head_of, kv_of):
    head = lax.broadcasted_iota(jnp.int32, vert_ref.shape, 1)
    weight = jnp.left_shift(1, head & 15).astype(f32)
    hit = jnp.where((vert_ref[...] >> 2) == shard, weight, 0.0)
    here = [
        jnp.sum(jnp.where((head >> 4) == part, hit, 0.0)).astype(jnp.int32) for part in range(2)
    ]
    for n in range(NS + 1):
        start[n] = 0
    for h in range(H):
        start[count_ref[h]] = start[count_ref[h]] + 1
    before = jnp.int32(0)
    for n in range(NS + 1):
        held = start[n]
        start[n] = before
        before = before + held
    groups = H // GROUP
    for h in range(H):
        rank = start[count_ref[h]]
        start[count_ref[h]] = rank + 1
        within = rank >> 3
        place = rank & (groups - 1)
        group = jnp.where((within & 1) == 0, place, groups - 1 - place)
        head_of[group * GROUP + within] = h
        kv_of[jnp.where(((here[h >> 4] >> (h & 15)) & 1) == 1, group, groups)] = h // (H // KVH)


def entry_kernel(count_ref, vert_ref, q_ref, kv_ref, out_ref, start, head_of, kv_of):
    lo = lax.axis_index("lo")
    zl = lo >> 3
    shard = (lax.axis_index("y") * NK + lax.axis_index("k")) * 2 + zl
    for g in range(KVH):
        kv_of[g] = 0
    entry_tables(count_ref, vert_ref, shard, start, head_of, kv_of)

    def q_cols(head):
        return q_ref[:, pl.ds(pl.multiple_of(head * DH, DH), DH)]

    def kv_cols(which, head):
        return kv_ref[:, pl.ds(pl.multiple_of(which * KVH * DH + head * DH, DH), DH)]

    for g in range(KVH):
        kv_head = kv_of[g]
        near = [kv_cols(0, kv_head), kv_cols(1, kv_head), kv_cols(0, g), kv_cols(1, g)]
        far = [q_cols(head_of[g * GROUP + p]) for p in range(GROUP)]
        for core, parts in ((zl, near), (1 - zl, far)):
            own = [q_cols(4 * g + 2 * core + a) for a in range(2)]
            for n, part in enumerate(parts + own):
                out_ref[2 * g + core, n * ROWS : (n + 1) * ROWS, :] = part


def pick_kernel(meta, in_ref, spread_ref, swap_ref, kv_ref):
    c = meta[M_LO] & 1
    half = LO // 2
    first = c * half + 2 * meta[M_BLOCK]
    for side in range(2):
        for which in range(2):
            part = in_ref[first + side, VERT + which * ROWS : VERT + (which + 1) * ROWS, :]
            at = which * BLOCK + side * ROWS
            for d in range(HI):
                spread_ref[d, at : at + ROWS, :] = part
    kv = in_ref[pl.ds(c * half, half), KVNAT:QNAT, :]
    kv_ref[...] = kv
    swap_ref[:, 0:KV_ROWS, :] = kv
    swap_ref[:, KV_ROWS:, :] = in_ref[pl.ds((1 - c) * half, half), QDYN:QNAT, :]


def scores(q, k):
    return lax.dot_general(q, k, (((1,), (1,)), ((), ())), preferred_element_type=f32)


def slash_kernel(
    meta, in_ref, swap_ref, before_ref, before_swap_ref, out_ref, stats_ref, q_ref, k_buf, v_buf
):
    lo = meta[M_LO]
    core = lo & 1
    some = LO // 2
    shard = some * ROWS
    pair = 2 * shard
    mine = pl.multiple_of(core * shard, shard)
    other = pl.multiple_of((1 - core) * shard, shard)
    far = pl.ds((1 - core) * some, some)
    near = pl.ds(core * some, some)
    for p in range(GROUP):
        rows = slice(p * ROWS, (p + 1) * ROWS)
        q_ref[p, pl.ds(other, shard), :] = in_ref[far, rows, :].reshape(shard, DH)
        rows = slice(KV_ROWS + p * ROWS, KV_ROWS + (p + 1) * ROWS)
        q_ref[p, pl.ds(mine, shard), :] = swap_ref[:, rows, :].reshape(shard, DH)
    for n, buf in enumerate((k_buf, v_buf)):
        rows = slice(n * ROWS, (n + 1) * ROWS)
        buf[pl.ds(mine, shard), :] = before_ref[:, rows, :].reshape(shard, DH)
        buf[pl.ds(other, shard), :] = before_swap_ref[:, rows, :].reshape(shard, DH)
        held = slice(KVNAT + n * ROWS, KVNAT + (n + 1) * ROWS)
        buf[pl.ds(pair + mine, shard), :] = in_ref[near, held, :].reshape(shard, DH)
        buf[pl.ds(pair + other, shard), :] = swap_ref[:, rows, :].reshape(shard, DH)

    first_block = meta[M_HI] * 8
    band = 8 * BLOCK
    offset = 8 - lax.broadcasted_iota(jnp.int32, (1, band), 1) // BLOCK
    causal = jnp.where(
        lax.broadcasted_iota(jnp.int32, (BLOCK, BLOCK), 1)
        <= lax.broadcasted_iota(jnp.int32, (BLOCK, BLOCK), 0),
        0.0,
        -jnp.inf,
    )
    lane = lax.broadcasted_iota(jnp.int32, (BLOCK, DH), 1)
    live = []
    for a in range(2):
        mask = meta[M_MASK + 2 * lo + a]
        live.append((jnp.right_shift(jnp.full((1, band), mask, jnp.int32), offset) & 1) == 1)

    def step(i, _):
        at = pl.multiple_of(i * BLOCK, BLOCK)
        near_at = pl.multiple_of(i * BLOCK + band, BLOCK)
        reach = offset <= first_block + i
        two = pl.ds(2 * i, 2)
        q = jnp.concatenate(
            [
                in_ref[two, QNAT + a * ROWS : QNAT + (a + 1) * ROWS, :].reshape(BLOCK, DH)
                for a in range(2)
            ],
            axis=0,
        )
        far = scores(q, k_buf[pl.ds(at, band), :])
        near = scores(q, k_buf[pl.ds(near_at, BLOCK), :])
        tile = jnp.zeros((BLOCK, DH), f32)
        for a in range(2):
            rows = slice(a * BLOCK, (a + 1) * BLOCK)
            s_far = far[rows] + jnp.where(live[a] & reach, 0.0, -jnp.inf)
            s_near = near[rows] + causal
            top = jnp.maximum(
                jnp.max(s_far, axis=1, keepdims=True), jnp.max(s_near, axis=1, keepdims=True)
            )
            e_far = jnp.exp2((s_far - top) * EXP2_SCALE)
            e_near = jnp.exp2((s_near - top) * EXP2_SCALE)
            total = jnp.sum(e_far, axis=1, keepdims=True) + jnp.sum(e_near, axis=1, keepdims=True)
            acc = jnp.dot(
                e_far.astype(bf16), v_buf[pl.ds(at, band), :], preferred_element_type=f32
            ) + jnp.dot(
                e_near.astype(bf16), v_buf[pl.ds(near_at, BLOCK), :], preferred_element_type=f32
            )
            out_ref[two, a * ROWS : (a + 1) * ROWS, :] = acc.astype(bf16).reshape(2, ROWS, DH)
            tile = jnp.where(lane == GROUP + a, top, tile)
            tile = jnp.where(lane == L_LANE + GROUP + a, total, tile)
        stats_ref[two] = tile.reshape(2, ROWS, DH)
        return 0

    lax.fori_loop(0, 8, step, 0)


def vertical_kernel(
    meta,
    vert_ref,
    q_buf,
    all_ref,
    slash_ref,
    slash_stats_ref,
    out_ref,
    k_buf,
    v_buf,
    stats_buf,
    bias_buf,
):
    lo = meta[M_LO]
    g = lo >> 1
    c = lo & 1
    first_block = meta[M_HI] * 8
    tokens = LO * ROWS
    width = NV * BLOCK
    out_ref[:, OS:STATS, :] = slash_ref[...]
    stats_buf[...] = slash_stats_ref[...].reshape(tokens, DH)
    k_buf[...] = jnp.zeros(k_buf.shape, bf16)
    v_buf[...] = jnp.zeros(v_buf.shape, bf16)
    of_lane = lax.broadcasted_iota(jnp.int32, (1, width), 1) // BLOCK

    def head_step(p, _):
        head = meta[M_HEAD + g * GROUP + p]
        count = jnp.int32(0)
        ids = jnp.full((1, width), 1 << 20, jnp.int32)
        for j in range(NV):
            v = vert_ref[j, head]
            mine = ((v >> 2) & 1) == c
            source = v >> 3
            at = pl.multiple_of(count * BLOCK, BLOCK)
            k_buf[pl.ds(at, BLOCK), :] = all_ref[source, 0:BLOCK, :]
            v_buf[pl.ds(at, BLOCK), :] = all_ref[source, BLOCK : 2 * BLOCK, :]
            ids = jnp.where(of_lane == jnp.where(mine, count, NV), v, ids)
            count = count + mine.astype(jnp.int32)
        block_of_row = lax.broadcasted_iota(jnp.int32, (8, width), 0) + first_block
        distance = block_of_row - ids
        mask = jnp.full((8, width), meta[M_MASK + head], jnp.int32)
        slashed = jnp.right_shift(mask, jnp.clip(distance, 0, 31)) & 1
        bias_buf[...] = jnp.where((distance > 0) & (slashed == 0), 0.0, -jnp.inf)

        def attend(n):
            size = n * BLOCK

            rows = LO * ROWS // STEPS
            lane = lax.broadcasted_iota(jnp.int32, (rows, DH), 1)
            for i in range(STEPS):
                span = slice(i * rows, (i + 1) * rows)
                s = scores(q_buf[p, span, :], k_buf[0:size, :])
                parts = []
                for t in range(rows // BLOCK):
                    at = i * (rows // BLOCK) + t
                    bias = bias_buf[at : at + 1, 0:size]
                    parts.append(s[t * BLOCK : (t + 1) * BLOCK] + bias)
                s = jnp.concatenate(parts, axis=0)
                top = jnp.maximum(jnp.max(s, axis=1, keepdims=True), LOWEST)
                e = jnp.exp2((s - top) * EXP2_SCALE)
                total = jnp.sum(e, axis=1, keepdims=True)
                acc = jnp.dot(e.astype(bf16), v_buf[0:size, :], preferred_element_type=f32)
                held = slice(i * rows // ROWS, (i + 1) * rows // ROWS)
                out_ref[held, pl.ds(pl.multiple_of(OV + p * ROWS, ROWS), ROWS), :] = acc.astype(
                    bf16
                ).reshape(rows // ROWS, ROWS, DH)
                tile = jnp.where(lane == p, top, stats_buf[span, :])
                stats_buf[span, :] = jnp.where(lane == L_LANE + p, total, tile)

        for low, n in ((-1, 8), (8, 12), (12, 16)):

            @pl.when((count > low) & (count <= n))
            def _(n=n):
                attend(n)

        return 0

    lax.fori_loop(0, GROUP, head_step, 0)
    stats = stats_buf[...]
    first = stats.astype(bf16).astype(f32)
    stats = stats - first
    second = stats.astype(bf16).astype(f32)
    third = stats - second
    packed = first + pltpu.roll(second, PART, 1) + pltpu.roll(third, 2 * PART, 1)
    packed = packed.reshape(LO, ROWS, DH)
    low = packed[:, 0 : ROWS // 2, :].reshape(LO * ROWS // 2, DH)
    high = packed[:, ROWS // 2 :, :].reshape(LO * ROWS // 2, DH)
    packed = low + pltpu.roll(high, DH // 2, 1)
    out_ref[:, STATS:, :] = packed.astype(bf16).reshape(LO, ROWS // 2, DH)


def exit_kernel(meta, in_ref, gate_ref, out_ref, m_buf, l_buf):
    row = lax.broadcasted_iota(jnp.int32, (DH, DH), 0)
    value = jnp.where(row < 3 * PART, row & (PART - 1), PART)
    stats = in_ref[:, STATS:, :].reshape(LO * ROWS // 2, DH)
    turned = pltpu.roll(stats.astype(f32), DH // 2, 1).astype(bf16)
    for buf, lane in ((m_buf, 0), (l_buf, L_LANE)):
        pick = jnp.concatenate(
            [jnp.where(value == lane + n, 1.0, 0.0).astype(bf16) for n in range(SLOTS)], axis=1
        )
        for side, part in enumerate((stats, turned)):
            held = slice(side * ROWS // 2, (side + 1) * ROWS // 2)
            buf[:, held, :] = jnp.dot(part, pick, preferred_element_type=f32).reshape(
                LO, ROWS // 2, SLOTS * DH
            )

    for n in range(LO):
        for a in range(2):
            h = 2 * n + a
            cols = slice((GROUP + a) * DH, (GROUP + a + 1) * DH)
            tops = [m_buf[n, :, cols]]
            sums = [l_buf[n, :, cols]]
            accs = [in_ref[n, OS + a * ROWS : OS + (a + 1) * ROWS, :]]
            slot = meta[M_SLOT + h]
            p = slot & 3
            lanes = pl.ds(pl.multiple_of(p * DH, DH), DH)
            for c in range(2):
                source = 2 * (slot >> 2) + c
                tops.append(m_buf[source, :, lanes])
                sums.append(l_buf[source, :, lanes])
                accs.append(in_ref[source, pl.ds(pl.multiple_of(OV + p * ROWS, ROWS), ROWS), :])
            best = jnp.maximum(jnp.maximum(tops[0], tops[1]), tops[2])
            num = jnp.zeros((ROWS, DH), f32)
            den = jnp.zeros((ROWS, DH), f32)
            for top, total, acc in zip(tops, sums, accs):
                w = jnp.exp2((top - best) * EXP2_SCALE)
                num = num + w * acc.astype(f32)
                den = den + w * total
            attended = (num / den).astype(bf16).astype(f32)
            at = slice(h * DH, (h + 1) * DH)
            gate = gate_ref[:, at].astype(f32)
            out_ref[:, at] = (jax.nn.sigmoid(gate) * attended).astype(bf16)


def call(kernel, out_shape, in_specs, scratch=(), **options):
    run = pl.pallas_call(
        kernel,
        out_shape=out_shape,
        in_specs=in_specs,
        out_specs=tuple(VMEM for _ in out_shape) if isinstance(out_shape, tuple) else VMEM,
        scratch_shapes=list(scratch),
        **options,
    )

    def placed(*args):
        return run(
            *(
                pltpu.with_memory_space_constraint(arg, pltpu.VMEM) if spec is VMEM else arg
                for arg, spec in zip(args, in_specs)
            )
        )

    return placed


def shape(rows, dtype=bf16, lead=LO):
    return jax.ShapeDtypeStruct((lead, rows, DH), dtype)


def in_vmem(rows, lead=LO):
    return pltpu.VMEM((lead, rows, DH), bf16)


def body(queries, key_values, gate_logits, vertical_blocks, slash_offsets, slash_count):
    meta = tables(vertical_blocks, slash_offsets, slash_count)
    vertical_ids = vertical_blocks.T
    flat_kv = key_values.reshape(ROWS, 2 * KVH * DH)
    sent = call(
        entry_kernel,
        shape(IN_ROWS),
        [SMEM, LOADED, VMEM, VMEM],
        [pltpu.SMEM((16,), jnp.int32), pltpu.SMEM((H,), jnp.int32), pltpu.SMEM((16,), jnp.int32)],
    )(slash_count, vertical_ids, queries, flat_kv)
    mine = lax.all_to_all(sent, "lo", 0, 0, tiled=True)
    spread, swap, kv_own = call(
        pick_kernel,
        (
            shape(2 * BLOCK, lead=HI),
            in_vmem(KV_ROWS + QNAT, lead=LO // 2),
            in_vmem(KV_ROWS, lead=LO // 2),
        ),
        [SMEM, VMEM],
    )(meta, mine)
    before = lax.ppermute(kv_own, ("y", "k"), [(i, i + 1) for i in range(HI - 1)])
    verticals = lax.all_to_all(spread, ("y", "k"), 0, 0, tiled=True)
    partner = [(i, i ^ 1) for i in range(LO)]
    swapped = lax.ppermute(swap, "lo", partner)
    before_swap = lax.ppermute(before, "lo", partner)
    slash, slash_stats, vertical_queries = call(
        slash_kernel,
        (shape(2 * ROWS), shape(ROWS, f32), shape(LO * ROWS, lead=GROUP)),
        [SMEM, VMEM, VMEM, VMEM, VMEM],
        [pltpu.VMEM((2 * LO * ROWS, DH), bf16)] * 2,
    )(meta, mine, swapped, before, before_swap)
    partial = call(
        vertical_kernel,
        in_vmem(OUT_ROWS),
        [SMEM, SMEM, LOADED, VMEM, LOADED, LOADED],
        [
            pltpu.VMEM(((NV + 1) * BLOCK, DH), bf16),
            pltpu.VMEM(((NV + 1) * BLOCK, DH), bf16),
            pltpu.VMEM((LO * ROWS, DH), f32),
            pltpu.VMEM((8, NV * BLOCK), f32),
        ],
    )(meta, vertical_ids, vertical_queries, verticals, slash, slash_stats)
    back = lax.all_to_all(partial, "lo", 0, 0, tiled=True)
    return call(
        exit_kernel,
        jax.ShapeDtypeStruct((ROWS, H * DH), bf16),
        [SMEM, VMEM, VMEM],
        [pltpu.VMEM((LO, ROWS, SLOTS * DH), f32)] * 2,
    )(meta, back, gate_logits)


def solution(mesh):
    pairs = Mesh(mesh.devices.reshape(NY, NK, LO), ("y", "k", "lo"))
    tokens = P(("y", "k", "lo"))

    return jax.shard_map(
        body,
        mesh=pairs,
        in_specs=(tokens, tokens, tokens, P(), P(), P()),
        out_specs=tokens,
        check_vma=False,
    )
```
